32 devices in a mesh: dp: 8 (over y, x, core), seq: 4 (over z).
Axes of the slice: x: 2, y: 2, z: 4, core: 2. Of those that a mesh axis runs over, the one named last changes fastest.
Arguments:
- tokens: bfloat16 [24, 736, 1152], P('dp', 'seq'), may hold values from -6 to 6
- out_grad: bfloat16 [24, 736, 1152], P('dp', 'seq'), may hold values from -6 to 6
- image_count: int32 [8], P('dp'), may hold values from 1 to 3, 18 in all
- adapter_id: int32 [24], P('dp'), may hold values from 0 to 7
- key_live: int32 [24, 736], P('dp'), may hold values from 0 to 1, as said below
- w_qkv: bfloat16 [1152, 3, 1152], P('seq'), may hold values from -0.1875 to 0.1875
- w_out: bfloat16 [1152, 1152], P('seq'), may hold values from -0.75 to 0.75
- w_fc1: bfloat16 [1152, 4304], P('seq'), may hold values from -0.1875 to 0.1875
- w_fc2: bfloat16 [4304, 1152], P('seq'), may hold values from -0.09375 to 0.09375
- norm_gain: float32 [2, 1152], replicated, may hold values from 0.25 to 1.75
- norm_bias: float32 [2, 1152], replicated, may hold values from -2 to 2
- proj_bias: float32 [4, 1152], replicated, may hold values from -2 to 2
- hidden_bias: float32 [4304], replicated, may hold values from -3 to 3
- down_attn: bfloat16 [4, 1152, 128], replicated, may hold values from -0.1875 to 0.1875
- up_attn: bfloat16 [4, 128, 1152], replicated, may hold values from -1.5 to 1.5
- down_fc1: bfloat16 [1152, 128], replicated, may hold values from -0.1875 to 0.1875
- up_fc1: bfloat16 [128, 4304], replicated, may hold values from -1.5 to 1.5
- down_fc2: bfloat16 [4304, 128], replicated, may hold values from -0.09375 to 0.09375
- up_fc2: bfloat16 [128, 1152], replicated, may hold values from -1.5 to 1.5
Outputs:
- layer_out: bfloat16 [24, 736, 1152], P('dp', 'seq')
- input_grad: float32 [24, 736, 1152], P('dp', 'seq')
- down_attn_grad: float32 [4, 1152, 128], replicated
- up_attn_grad: float32 [4, 128, 1152], replicated
- down_fc1_grad: float32 [1152, 128], replicated
- up_fc1_grad: float32 [128, 4304], replicated
- down_fc2_grad: float32 [4304, 128], replicated
- up_fc2_grad: float32 [128, 1152], replicated
The draws below stay inside these ranges and needn't reach their ends.
Inputs may be any that keep to these rules, and one draw needn't show every extreme that they name: Group g of 3 image slots holds image_count[g] live images, in its first slots; the counts sum to 18, and some group is full. `key_live`: each image has exactly 7 pad slots, at positions drawn per image.
All inputs are finite; a program needn't handle non-finite values.
Results may differ from the reference program's by a relative error of at most 0.015.
The reference program's roundings to bfloat16 on the way count: a program that leaves them out, or rounds other values in their place, can miss the bound.
Values may be sent and summed in bfloat16 or wider, within the bound.
No kernel may reach another device: no remote copies, remote signals or barrier semaphores. Data moves between devices by JAX's collectives and lax.ppermute only.
A program may use at most 192 MiB of HBM per device.

```python
import math
import jax
import jax.numpy as jnp
import numpy as np
from jax import lax

D = 1152
HEADS = 16
HD = 72
FF = 4304
SEQ = 736
PADS = 7
ADAPT = 8
RANK = 16
IMG_DEV = 3
IMAGES = 24
N_DP = 8


def draw_key_live(key, part):
    noise = jax.random.randint(key, (IMAGES, SEQ), 0, 1048576, dtype=jnp.int32)
    distinct = noise * SEQ + jnp.arange(SEQ, dtype=jnp.int32)[None, :]
    ordering = jnp.argsort(distinct, axis=1)
    ranking = jnp.argsort(ordering, axis=1)
    return (ranking >= PADS).astype(jnp.int32)


def set_ends(entries, own_key, smallest, top_value):
    index_at = [jax.random.randint(jax.random.fold_in(own_key, axis), (), 0, length) for axis, length in enumerate(entries.shape)]
    widest = entries.shape.index(max(entries.shape))
    next_to = index_at[:widest] + [(index_at[widest] + 1) % entries.shape[widest]] + index_at[widest + 1:]
    return entries.at[tuple(index_at)].set(smallest).at[tuple(next_to)].set(top_value)


def levels(key, dims, shards, least, largest):
    factor_of = 1.0
    for axis_at, blocks in shards:
        heights = jax.random.uniform(jax.random.fold_in(jax.random.fold_in(key, 6), axis_at), (blocks,), jnp.float32, least / len(shards), largest / len(shards))
        factor_of = factor_of * jnp.repeat(jnp.exp(heights), dims[axis_at] // blocks).reshape((-1,) + (1,) * (len(dims) - 1 - axis_at))
    return factor_of


def split_up(number_of, total, limit, lean):
    portions = [(1 << 20) // math.isqrt(rank ** lean) + 1 for rank in range(2, number_of + 1)]
    surplus, holding = total - limit - (number_of - 1), [1] * (number_of - 1)
    while surplus > 0:
        candidates = [i for i in range(number_of - 1) if holding[i] < limit]
        mass, remaining = sum([portions[i] for i in candidates]), surplus
        for i in candidates:
            addition = min(limit - holding[i], max(1, remaining * portions[i] // mass), surplus)
            holding[i] = holding[i] + addition
            surplus = surplus - addition
    return np.array([limit] + holding)


def uneven(own_key, amount, total, reach, slope):
    if amount == 2:
        one = jax.random.randint(own_key, (), max(1, total - reach), min(reach, total - 1) + 1)
        return jnp.stack([one, total - one])
    sizes = jnp.asarray(split_up(amount, total, reach, slope), jnp.int32)
    pairs = (amount - 1) // 2
    donor, sink = sizes[1:1 + 2 * pairs:2], sizes[2:2 + 2 * pairs:2]
    margin = jnp.minimum(donor - 1, reach - sink)
    passed = jax.random.randint(jax.random.fold_in(own_key, 1), (pairs,), 0, 1 << 20) % (margin + 1)
    sizes = sizes.at[1:1 + 2 * pairs:2].set(donor - passed).at[2:2 + 2 * pairs:2].set(sink + passed)
    return sizes[jax.random.permutation(jax.random.fold_in(own_key, 2), amount)]


def scatter_about(key, dims, spread, reach, split=(), held_as=jnp.bfloat16):
    values = jax.random.normal(key, dims, jnp.float32) * spread
    if len(split) > 0:
        values = levels(key, dims, split, -0.22, 0.18) * values
    return jnp.clip(values, min=-reach, max=reach).astype(held_as)


def setup_inputs(seed: int = 0) -> dict:
    splits = jax.random.split(jax.random.key(seed), 20)
    return {
        "tokens": scatter_about(splits[0], (IMAGES, SEQ, D), 1.0, 6.0, ((0, 8), (1, 4))),
        "out_grad": scatter_about(splits[1], (IMAGES, SEQ, D), 1.0, 6.0, ((0, 8), (1, 4))),
        "image_count": uneven(splits[2], N_DP, N_DP * IMG_DEV * 3 // 4, IMG_DEV, 0).astype(jnp.int32),
        "adapter_id": set_ends(jax.random.randint(splits[3], (IMAGES,), 0, ADAPT), jax.random.fold_in(splits[3], 1), 0, ADAPT - 1).astype(jnp.int32),
        "key_live": draw_key_live(jax.random.fold_in(splits[19], 71), 0),
        "w_qkv": scatter_about(splits[5], (D, 3, D), D ** -0.5, 0.1875, ((0, 4),)),
        "w_out": scatter_about(splits[6], (D, D), (D // 16) ** -0.5, 0.75, ((0, 4),)),
        "w_fc1": scatter_about(splits[7], (D, FF), D ** -0.5, 0.1875, ((0, 4),)),
        "w_fc2": scatter_about(splits[8], (FF, D), FF ** -0.5, 0.09375, ((0, 4),)),
        "norm_gain": jnp.clip(1.0 + 0.15 * jax.random.normal(splits[9], (2, D), jnp.float32), 0.25, 1.75),
        "norm_bias": scatter_about(splits[10], (2, D), 0.3, 2.0, (), jnp.float32),
        "proj_bias": scatter_about(splits[11], (4, D), 0.3, 2.0, (), jnp.float32),
        "hidden_bias": scatter_about(splits[12], (FF,), 0.5, 3.0, (), jnp.float32),
        "down_attn": scatter_about(splits[13], (4, D, ADAPT * RANK), D ** -0.5, 0.1875),
        "up_attn": scatter_about(splits[14], (4, ADAPT * RANK, D), RANK ** -0.5, 1.5),
        "down_fc1": scatter_about(splits[15], (D, ADAPT * RANK), D ** -0.5, 0.1875),
        "up_fc1": scatter_about(splits[16], (ADAPT * RANK, FF), RANK ** -0.5, 1.5),
        "down_fc2": scatter_about(splits[17], (FF, ADAPT * RANK), FF ** -0.5, 0.09375),
        "up_fc2": scatter_about(splits[18], (ADAPT * RANK, D), RANK ** -0.5, 1.5),
    }


@jax.custom_vjp
def low(v):
    return lax.optimization_barrier(v.astype(jnp.bfloat16)).astype(jnp.float32)

@jax.custom_vjp
def low_back(v):
    return v

def low_keep(v):
    return (low(v), None)

def low_pass(kept, grad):
    return (grad,)

def back_keep(v):
    return (v, None)

def back_low(kept, grad):
    return (low(grad),)
low.defvjp(low_keep, low_pass)
low_back.defvjp(back_keep, back_low)
norm_eps = 1e-06
top_precision = lax.Precision.HIGHEST

def matmul(left, right):
    return jnp.matmul(left, right, precision=top_precision)

def layer_norm(values, gain, shift):
    average = lax.optimization_barrier(jnp.mean(values, axis=-1, keepdims=True))
    centred = values - average
    variance = lax.optimization_barrier(jnp.mean(centred * centred, axis=-1, keepdims=True))
    return centred * lax.rsqrt(variance + norm_eps) * gain + shift

def adapted(inputs, weight, down_factor, up_factor, select):
    inner_rank = matmul(inputs, down_factor)
    rank_part = low(low_back(inner_rank * select))
    return matmul(inputs, weight) + matmul(rank_part, up_factor)

def attend_image(operands):
    queries, key_rows, value_rows, key_mask = operands
    scores = jnp.einsum('qhd,khd->hqk', queries, key_rows, precision=top_precision) * HD ** (-0.5)
    scores = low_back(scores)
    scores = jnp.where(key_mask[None, None, :] > 0, scores, -1e+30)
    attn_probs = low(jax.nn.softmax(scores, axis=-1))
    return jnp.einsum('hqk,khd->qhd', attn_probs, value_rows, precision=top_precision)

def layer_forward(inputs, factor_set, weights, select, live, key_live):
    down_attn, up_attn, down_fc1, up_fc1, down_fc2, up_fc2 = factor_set
    w_qkv, w_out, w_fc1, w_fc2, norm_gain, norm_bias, proj_bias, hidden_bias = weights
    normed = low(layer_norm(inputs, norm_gain[0], norm_bias[0]))
    queries = adapted(normed, w_qkv[:, 0, :], down_attn[0], up_attn[0], select) + proj_bias[0]
    key_rows = adapted(normed, w_qkv[:, 1, :], down_attn[1], up_attn[1], select)
    value_rows = adapted(normed, w_qkv[:, 2, :], down_attn[2], up_attn[2], select) + proj_bias[1]
    head_shape = (IMAGES, SEQ, HEADS, HD)
    queries = low_back(low(queries)).reshape(head_shape)
    key_rows = low_back(low(key_rows)).reshape(head_shape)
    value_rows = low_back(low(value_rows)).reshape(head_shape)
    attended = lax.map(jax.checkpoint(attend_image), (queries, key_rows, value_rows, key_live))
    merged = low_back(low(attended.reshape(IMAGES, SEQ, D)))
    branch = adapted(merged, w_out, down_attn[3], up_attn[3], select) + proj_bias[2]
    resid = inputs + low_back(branch)
    normed_two = low(layer_norm(resid, norm_gain[1], norm_bias[1]))
    hidden = low_back(adapted(normed_two, w_fc1, down_fc1, up_fc1, select) + hidden_bias)
    activated = low(jax.nn.gelu(hidden, approximate=True))
    branch_two = adapted(activated, w_fc2, down_fc2, up_fc2, select) + proj_bias[3]
    return (resid + low_back(branch_two)) * live

def reference(tokens, out_grad, image_count, adapter_id, key_live, w_qkv, w_out, w_fc1, w_fc2, norm_gain, norm_bias, proj_bias, hidden_bias, down_attn, up_attn, down_fc1, up_fc1, down_fc2, up_fc2):
    image_slot = jnp.arange(IMAGES, dtype=jnp.int32)
    group_count = image_count[image_slot // IMG_DEV]
    live = (image_slot % IMG_DEV < group_count).astype(jnp.float32)[:, None, None]
    columns = jnp.arange(ADAPT * RANK, dtype=jnp.int32) // RANK
    select = (columns[None, :] == adapter_id[:, None]).astype(jnp.float32)[:, None, :]
    weights = tuple((item.astype(jnp.float32) for item in (w_qkv, w_out, w_fc1, w_fc2, norm_gain, norm_bias, proj_bias, hidden_bias)))
    factors = tuple((item.astype(jnp.float32) for item in (down_attn, up_attn, down_fc1, up_fc1, down_fc2, up_fc2)))

    def wrapped(inputs, factor_set):
        return layer_forward(inputs, factor_set, weights, select, live, key_live)
    result, pullback = jax.vjp(wrapped, tokens.astype(jnp.float32), factors)
    input_grad, factor_grads = pullback(out_grad.astype(jnp.float32))
    return (result.astype(jnp.bfloat16), input_grad, factor_grads[0], factor_grads[1], factor_grads[2], factor_grads[3], factor_grads[4], factor_grads[5])
```

```python
import jax
import jax.numpy as jnp
from jax import lax
from jax.sharding import PartitionSpec as P

HD = 72
RANK = 16
BF = jnp.bfloat16
F32 = jnp.float32

norm_eps = 1e-06


def dot(left, right, dims):
    return lax.dot_general(left, right, (dims, ((), ())), preferred_element_type=F32)


def product(left, right):
    return dot(left, right, ((1,), (0,)))


def product_back(grad, weight):
    return dot(grad, weight, ((1,), (1,)))


def outer_sum(left, right):
    return dot(left, right, ((0,), (0,)))


def layer_norm(values, gain, shift):
    average = jnp.mean(values, axis=-1, keepdims=True)
    centred = values - average
    variance = jnp.mean(centred * centred, axis=-1, keepdims=True)
    return centred * lax.rsqrt(variance + norm_eps) * gain + shift


def norm_back(values, gain, shift, grad):

    def local_norm(inner_values):
        return layer_norm(inner_values, gain, shift)

    return jax.vjp(local_norm, values)[1](grad)[0]


def gelu_tanh(values):
    return jax.nn.gelu(values, approximate=True)


def attend_heads(operands):
    queries, key_rows, value_rows, key_mask = operands
    scores = jnp.einsum(
        "qhd,khd->hqk", queries, key_rows, preferred_element_type=F32
    ) * HD ** (-0.5)
    scores = jnp.where(key_mask[None, None, :] > 0, scores, -1e30)
    row_top = jnp.max(scores, axis=-1, keepdims=True)
    exponent = jnp.exp(scores - row_top)
    row_total = jnp.sum(exponent, axis=-1, keepdims=True)
    attn_probs = (exponent / row_total).astype(BF)
    output = jnp.einsum("hqk,khd->qhd", attn_probs, value_rows, preferred_element_type=F32)
    return (output, (row_top + jnp.log(row_total))[:, :, 0])


def attend_back(operands):
    queries, key_rows, value_rows, key_mask, log_total, grad_out = operands
    scores = jnp.einsum(
        "qhd,khd->hqk", queries, key_rows, preferred_element_type=F32
    ) * HD ** (-0.5)
    scores = jnp.where(key_mask[None, None, :] > 0, scores, -1e30)
    attn_probs = jnp.exp(scores - log_total[:, :, None])
    grad_values = jnp.einsum(
        "hqk,qhd->khd", attn_probs.astype(BF), grad_out, preferred_element_type=F32
    )
    grad_probs = jnp.einsum("qhd,khd->hqk", grad_out, value_rows, preferred_element_type=F32)
    row_dot = jnp.sum(attn_probs * grad_probs, axis=-1, keepdims=True)
    grad_scores = (attn_probs * (grad_probs - row_dot)).astype(BF)
    grad_queries = jnp.einsum(
        "hqk,khd->qhd", grad_scores, key_rows, preferred_element_type=F32
    ) * HD ** (-0.5)
    grad_keys = jnp.einsum(
        "hqk,qhd->khd", grad_scores, queries, preferred_element_type=F32
    ) * HD ** (-0.5)
    return (grad_queries.astype(BF), grad_keys.astype(BF), grad_values.astype(BF))


class Place:
    def __init__(self, dp_size, seq_size):
        self.dp_size = dp_size
        self.seq_size = seq_size
        self.dp = lax.axis_index("dp")
        self.seq = lax.axis_index("seq")
        self.slot = self.image_of(self.dp, self.seq)

    def image_of(self, dp, seq):
        last = self.seq_size - 1
        if isinstance(dp, int):
            return last - seq if dp % 2 else seq
        return jnp.where(dp % 2 == 1, last - seq, seq)

    def flip(self, values, bit):
        pairs = [(n, n ^ bit) for n in range(self.dp_size)]
        return lax.ppermute(values, "dp", pairs)

    def to_image(self, values):
        images, length, width = values.shape
        size = self.seq_size
        full = jnp.zeros((size, length, width), values.dtype)
        for step in range(size):
            slot = jnp.minimum(self.image_of(self.dp, (self.seq + step) % size), images - 1)
            part = lax.dynamic_slice(values, (slot, 0, 0), (1, length, width))
            if step:
                pairs = []
                for dp in range(self.dp_size):
                    for seq in range(size):
                        target = (seq + step) % size
                        if self.image_of(dp, target) < images:
                            pairs.append((dp * size + seq, dp * size + target))
                part = lax.ppermute(part, ("dp", "seq"), pairs)
            full = lax.dynamic_update_slice(full, part, ((self.seq - step) % size, 0, 0))
        return full.reshape(size * length, width)

    def to_tokens(self, values, images):
        size = self.seq_size
        length = values.shape[0] // size
        width = values.shape[1]
        blocks = values.reshape(size, length, width)
        full = jnp.zeros((size, length, width), values.dtype)
        for step in range(size):
            part = lax.dynamic_slice(
                blocks, ((self.seq + step) % size, 0, 0), (1, length, width)
            )
            if step:
                pairs = []
                for dp in range(self.dp_size):
                    for seq in range(size):
                        if self.image_of(dp, seq) < images:
                            pairs.append((dp * size + seq, dp * size + (seq + step) % size))
                part = lax.ppermute(part, ("dp", "seq"), pairs)
            slot = self.image_of(self.dp, (self.seq - step) % size)
            full = lax.dynamic_update_slice(full, part, (slot, 0, 0))
        return full[:images]

    def gather_pieces(self, piece):
        rows, width = piece.shape
        size = self.seq_size
        half = size // 2
        own = lax.all_gather(piece, "seq", axis=0)
        over_x = self.flip(own, 2)
        over_y = self.flip(own, 4)
        corner_a = self.flip(over_x[:half], 4)
        corner_b = self.flip(over_y[half:], 2)
        full = jnp.zeros((8, size, rows, width), piece.dtype)
        at = self.dp % 8
        for part, mask, start in (
            (own, 0, 0),
            (over_x, 2, 0),
            (over_y, 4, 0),
            (corner_a, 6, 0),
            (corner_b, 6, half),
        ):
            other = self.flip(part, 1)
            full = lax.dynamic_update_slice(full, part[None], (at ^ mask, start, 0, 0))
            full = lax.dynamic_update_slice(full, other[None], (at ^ mask ^ 1, start, 0, 0))
        return full


def pad_blocks(values, axis, blocks, padded):
    shape = values.shape
    size = shape[axis] // blocks
    values = values.reshape(shape[:axis] + (blocks, size) + shape[axis + 1 :])
    pads = [(0, 0)] * values.ndim
    pads[axis + 1] = (0, padded - size)
    values = jnp.pad(values, pads)
    return values.reshape(shape[:axis] + (blocks * padded,) + shape[axis + 1 :])


def cut_blocks(values, axis, blocks, size):
    shape = values.shape
    padded = shape[axis] // blocks
    values = values.reshape(shape[:axis] + (blocks, padded) + shape[axis + 1 :])
    values = lax.slice_in_dim(values, 0, size, axis=axis + 1)
    return values.reshape(shape[:axis] + (blocks * size,) + shape[axis + 1 :])


def sum_images(parts, owner, devices):
    joined = jnp.concatenate(parts, axis=1).astype(BF)
    rank, total = joined.shape
    width = -(-total // (devices * 128)) * 128
    joined = jnp.pad(joined, ((0, 0), (0, devices * width - total)))
    pieces = joined.reshape(rank, devices, width).transpose(1, 0, 2)
    pieces = lax.all_to_all(pieces, ("dp", "seq"), split_axis=0, concat_axis=0, tiled=True)
    sums = dot(owner, pieces.reshape(devices, rank * width), ((0,), (0,))).astype(BF)
    sums = sums.reshape(-1, width)
    full = lax.all_gather(sums, ("dp", "seq"), axis=0)
    full = full.transpose(1, 0, 2).reshape(sums.shape[0], devices * width).astype(F32)
    out = []
    start = 0
    for part in parts:
        out.append(full[:, start : start + part.shape[1]])
        start += part.shape[1]
    return out


def local(
    dp_size,
    seq_size,
    tokens,
    out_grad,
    image_count,
    adapter_id,
    key_live,
    w_qkv,
    w_out,
    w_fc1,
    w_fc2,
    norm_gain,
    norm_bias,
    proj_bias,
    hidden_bias,
    down_attn,
    up_attn,
    down_fc1,
    up_fc1,
    down_fc2,
    up_fc2,
):
    images, local_len, width = tokens.shape
    rows = width // seq_size
    hidden_size = hidden_bias.shape[0]
    columns = down_attn.shape[-1]
    adapters = columns // RANK
    devices = dp_size * seq_size
    place = Place(dp_size, seq_size)
    own_slot = jnp.minimum(place.slot, images - 1)
    is_live = (place.slot < image_count[0]) & (place.slot < images)
    live = is_live.astype(F32)
    adapter = lax.dynamic_index_in_dim(adapter_id, own_slot, keepdims=False)
    key_mask = lax.dynamic_index_in_dim(key_live, own_slot, keepdims=False)
    owner = jnp.where(is_live & (jnp.arange(adapters) == adapter), 1.0, 0.0)
    owner = lax.all_gather(owner.astype(BF)[None], ("dp", "seq"), axis=0, tiled=True)

    part8 = place.dp % 8
    core = part8 % 2
    plane = part8 // 2
    joined = jnp.concatenate([w_qkv, w_out[:, None, :]], axis=1)
    piece = lax.dynamic_slice(joined, (core * (rows // 2), plane, 0), (rows // 2, 1, width))
    attn_full = place.gather_pieces(piece.reshape(rows // 2, width))
    attn_full = attn_full.reshape(4, 2, seq_size, rows // 2, width).transpose(0, 2, 1, 3, 4)
    attn_full = attn_full.reshape(4, width, width)

    shard = hidden_size // seq_size
    padded = -(-shard // 64) * 64
    hidden_pad = padded * seq_size
    fc1 = pad_blocks(w_fc1, 1, seq_size, padded)
    piece = lax.dynamic_slice(
        fc1, (plane * (rows // 4), core * (hidden_pad // 2)), (rows // 4, hidden_pad // 2)
    )
    fc1_full = place.gather_pieces(piece)
    fc1_full = fc1_full.reshape(4, 2, seq_size, rows // 4, hidden_pad // 2)
    fc1_full = fc1_full.transpose(2, 0, 3, 1, 4).reshape(width, hidden_pad)
    fc2 = jnp.pad(w_fc2, ((0, padded - shard), (0, 0)))
    piece = lax.dynamic_slice(fc2, (part8 * (padded // 8), 0), (padded // 8, width))
    fc2_full = place.gather_pieces(piece).transpose(1, 0, 2, 3).reshape(hidden_pad, width)

    def take(values, axis):
        return lax.dynamic_slice_in_dim(values, adapter * RANK, RANK, axis=axis)

    down_a = take(down_attn, 2)
    up_a = take(up_attn, 1)
    down_1 = take(down_fc1, 1)
    up_1 = pad_blocks(take(up_fc1, 0), 1, seq_size, padded)
    down_2 = pad_blocks(take(down_fc2, 1), 0, seq_size, padded)
    up_2 = take(up_fc2, 0)
    bias_1 = pad_blocks(hidden_bias, 0, seq_size, padded)

    flat = place.to_image(tokens).astype(F32)
    top_grad = place.to_image(out_grad).astype(F32) * live
    full_len = flat.shape[0]
    heads = width // HD

    normed = layer_norm(flat, norm_gain[0], norm_bias[0]).astype(BF)
    rank_parts = []
    projected = []
    for index in range(3):
        rank_part = product(normed, down_a[index]).astype(BF)
        rank_parts.append(rank_part)
        projected.append(product(normed, attn_full[index]) + product(rank_part, up_a[index]))
    queries = (projected[0] + proj_bias[0]).astype(BF)
    key_rows = projected[1].astype(BF)
    value_rows = (projected[2] + proj_bias[1]).astype(BF)

    groups = 4

    def split_heads(values):
        values = values.reshape(full_len, groups, heads // groups, HD)
        return values.transpose(1, 0, 2, 3)

    def join_heads(values):
        return values.transpose(1, 0, 2, 3).reshape(full_len, width)

    split_q, split_k, split_v = split_heads(queries), split_heads(key_rows), split_heads(value_rows)
    masks = jnp.broadcast_to(key_mask[None], (groups, full_len))
    attended, log_total = lax.map(attend_heads, (split_q, split_k, split_v, masks))
    merged = join_heads(attended).astype(BF)
    rank_out = product(merged, down_a[3]).astype(BF)
    resid = flat + product(merged, attn_full[3]) + product(rank_out, up_a[3]) + proj_bias[2]
    normed_two = layer_norm(resid, norm_gain[1], norm_bias[1]).astype(BF)
    rank_one = product(normed_two, down_1).astype(BF)
    hidden = product(normed_two, fc1_full) + product(rank_one, up_1) + bias_1
    activated = gelu_tanh(hidden).astype(BF)
    rank_two = product(activated, down_2).astype(BF)
    branch_two = product(activated, fc2_full) + product(rank_two, up_2) + proj_bias[3]
    result = place.to_tokens(((resid + branch_two) * live).astype(BF), images)

    two_grad = top_grad.astype(BF)
    inner_two = product_back(two_grad, up_2).astype(BF)
    up_2_grad = outer_sum(rank_two, two_grad)
    down_2_grad = outer_sum(inner_two, activated)
    act_grad = product_back(two_grad, fc2_full) + product_back(inner_two, down_2)
    hidden_grad = jax.vjp(gelu_tanh, hidden)[1](act_grad)[0].astype(BF)
    inner_one = product_back(hidden_grad, up_1).astype(BF)
    up_1_grad = outer_sum(rank_one, hidden_grad)
    down_1_grad = outer_sum(inner_one, normed_two)
    normed_two_grad = product_back(hidden_grad, fc1_full) + product_back(inner_one, down_1)
    resid_grad = top_grad + norm_back(resid, norm_gain[1], norm_bias[1], normed_two_grad)
    branch_grad = resid_grad.astype(BF)
    inner_o = product_back(branch_grad, up_a[3]).astype(BF)
    up_o_grad = outer_sum(rank_out, branch_grad)
    down_o_grad = outer_sum(inner_o, merged)
    merged_grad = product_back(branch_grad, attn_full[3]) + product_back(inner_o, down_a[3])
    merged_grad = merged_grad.astype(BF)
    early = sum_images(
        [down_2_grad, up_1_grad, up_2_grad, down_1_grad, down_o_grad, up_o_grad], owner, devices
    )

    grad_q, grad_k, grad_v = lax.map(
        attend_back, (split_q, split_k, split_v, masks, log_total, split_heads(merged_grad))
    )
    proj_grads = (join_heads(grad_q), join_heads(grad_k), join_heads(grad_v))
    normed_grad = 0.0
    late_parts = []
    for index in range(3):
        inner = product_back(proj_grads[index], up_a[index]).astype(BF)
        late_parts.append(outer_sum(inner, normed))
        late_parts.append(outer_sum(rank_parts[index], proj_grads[index]))
        normed_grad = (
            normed_grad
            + product_back(proj_grads[index], attn_full[index])
            + product_back(inner, down_a[index])
        )
    late = sum_images(late_parts, owner, devices)
    input_grad = resid_grad + norm_back(flat, norm_gain[0], norm_bias[0], normed_grad)
    input_grad = place.to_tokens(input_grad.astype(BF), images).astype(F32)

    down_2_sum = cut_blocks(early[0], 1, seq_size, shard).T
    up_1_sum = cut_blocks(early[1], 1, seq_size, shard)
    down_attn_sum = jnp.stack([late[0].T, late[2].T, late[4].T, early[4].T])
    up_attn_sum = jnp.stack([late[1], late[3], late[5], early[5]])
    return (
        result,
        input_grad,
        down_attn_sum,
        up_attn_sum,
        early[3].T,
        up_1_sum,
        down_2_sum,
        early[2],
    )


def solution(mesh):
    in_specs = (
        P("dp", "seq", None),
        P("dp", "seq", None),
        P("dp"),
        P("dp"),
        P("dp", None),
        P("seq", None, None),
        P("seq", None),
        P("seq", None),
        P("seq", None),
        P(),
        P(),
        P(),
        P(),
        P(),
        P(),
        P(),
        P(),
        P(),
        P(),
    )
    out_specs = (P("dp", "seq", None), P("dp", "seq", None), P(), P(), P(), P(), P(), P())

    def run(*args):
        return local(mesh.shape["dp"], mesh.shape["seq"], *args)

    return jax.shard_map(run, mesh=mesh, in_specs=in_specs, out_specs=out_specs, check_vma=False)
```

```python
import jax
import jax.numpy as jnp
from jax import lax
from jax.experimental import pallas as pl
from jax.experimental.pallas import tpu as pltpu
from jax.sharding import PartitionSpec as P

HD = 72
RANK = 16
BF = jnp.bfloat16
F32 = jnp.float32

norm_eps = 1e-06


def dot(left, right, dims):
    return lax.dot_general(left, right, (dims, ((), ())), preferred_element_type=F32)


def product(left, right):
    return dot(left, right, ((1,), (0,)))


def product_back(grad, weight):
    return dot(grad, weight, ((1,), (1,)))


def outer_sum(left, right):
    return dot(left, right, ((0,), (0,)))


def layer_norm(values, gain, shift):
    average = jnp.mean(values, axis=-1, keepdims=True)
    centred = values - average
    variance = jnp.mean(centred * centred, axis=-1, keepdims=True)
    return centred * lax.rsqrt(variance + norm_eps) * gain + shift


def norm_back(values, gain, shift, grad):

    def local_norm(inner_values):
        return layer_norm(inner_values, gain, shift)

    return jax.vjp(local_norm, values)[1](grad)[0]


def gelu_tanh(values):
    return jax.nn.gelu(values, approximate=True)


def attend_heads(operands):
    queries, key_rows, value_rows, key_mask = operands
    scores = jnp.einsum(
        "qhd,khd->hqk", queries, key_rows, preferred_element_type=F32
    ) * HD ** (-0.5)
    scores = jnp.where(key_mask[None, None, :] > 0, scores, -1e30)
    row_top = jnp.max(scores, axis=-1, keepdims=True)
    exponent = jnp.exp(scores - row_top)
    row_total = jnp.sum(exponent, axis=-1, keepdims=True)
    attn_probs = (exponent / row_total).astype(BF)
    output = jnp.einsum("hqk,khd->qhd", attn_probs, value_rows, preferred_element_type=F32)
    return (output, (row_top + jnp.log(row_total))[:, :, 0])


def attend_back(operands):
    queries, key_rows, value_rows, key_mask, log_total, grad_out = operands
    scores = jnp.einsum(
        "qhd,khd->hqk", queries, key_rows, preferred_element_type=F32
    ) * HD ** (-0.5)
    scores = jnp.where(key_mask[None, None, :] > 0, scores, -1e30)
    attn_probs = jnp.exp(scores - log_total[:, :, None])
    grad_values = jnp.einsum(
        "hqk,qhd->khd", attn_probs.astype(BF), grad_out, preferred_element_type=F32
    )
    grad_probs = jnp.einsum("qhd,khd->hqk", grad_out, value_rows, preferred_element_type=F32)
    row_dot = jnp.sum(attn_probs * grad_probs, axis=-1, keepdims=True)
    grad_scores = (attn_probs * (grad_probs - row_dot)).astype(BF)
    grad_queries = jnp.einsum(
        "hqk,khd->qhd", grad_scores, key_rows, preferred_element_type=F32
    ) * HD ** (-0.5)
    grad_keys = jnp.einsum(
        "hqk,qhd->khd", grad_scores, queries, preferred_element_type=F32
    ) * HD ** (-0.5)
    return (grad_queries.astype(BF), grad_keys.astype(BF), grad_values.astype(BF))


class Place:
    def __init__(self, dp_size, seq_size):
        self.dp_size = dp_size
        self.seq_size = seq_size
        self.dp = lax.axis_index("dp")
        self.seq = lax.axis_index("seq")
        self.slot = self.image_of(self.dp, self.seq)

    def image_of(self, dp, seq):
        last = self.seq_size - 1
        if isinstance(dp, int):
            return last - seq if dp % 2 else seq
        return jnp.where(dp % 2 == 1, last - seq, seq)

    def flip(self, values, bit):
        pairs = [(n, n ^ bit) for n in range(self.dp_size)]
        return lax.ppermute(values, "dp", pairs)

    def to_image(self, values):
        images, length, width = values.shape
        size = self.seq_size
        full = jnp.zeros((size, length, width), values.dtype)
        for step in range(size):
            slot = jnp.minimum(self.image_of(self.dp, (self.seq + step) % size), images - 1)
            part = lax.dynamic_slice(values, (slot, 0, 0), (1, length, width))
            if step:
                pairs = []
                for dp in range(self.dp_size):
                    for seq in range(size):
                        target = (seq + step) % size
                        if self.image_of(dp, target) < images:
                            pairs.append((dp * size + seq, dp * size + target))
                part = lax.ppermute(part, ("dp", "seq"), pairs)
            full = lax.dynamic_update_slice(full, part, ((self.seq - step) % size, 0, 0))
        return full.reshape(size * length, width)

    def to_tokens(self, values, images):
        size = self.seq_size
        length = values.shape[0] // size
        width = values.shape[1]
        blocks = values.reshape(size, length, width)
        full = jnp.zeros((size, length, width), values.dtype)
        for step in range(size):
            part = lax.dynamic_slice(
                blocks, ((self.seq + step) % size, 0, 0), (1, length, width)
            )
            if step:
                pairs = []
                for dp in range(self.dp_size):
                    for seq in range(size):
                        if self.image_of(dp, seq) < images:
                            pairs.append((dp * size + seq, dp * size + (seq + step) % size))
                part = lax.ppermute(part, ("dp", "seq"), pairs)
            slot = self.image_of(self.dp, (self.seq - step) % size)
            full = lax.dynamic_update_slice(full, part, (slot, 0, 0))
        return full[:images]

    def gather_own(self, piece):
        return lax.all_gather(piece, "seq", axis=0)

    def gather_rest(self, own, shape, index):
        half = self.seq_size // 2
        over_x = self.flip(own, 2)
        over_y = self.flip(own, 4)
        corner_a = self.flip(over_x[:half], 4)
        corner_b = self.flip(over_y[half:], 2)
        parts = [own, over_x, over_y, corner_a, corner_b]
        masks = [0, 2, 4, 6, 6]
        starts = [0, 0, 0, 0, half]
        others = [self.flip(part, 1) for part in parts]
        at = (self.dp % 8).astype(jnp.int32).reshape(1)

        def body(at_ref, *refs):
            out_ref, sems = refs[-2], refs[-1]
            copies = []
            for n in range(10):
                part = at_ref[0] ^ (masks[n % 5] ^ (n // 5))
                rows = pl.ds(starts[n % 5], parts[n % 5].shape[0])
                target = out_ref.at[index(part, rows)]
                copies.append(pltpu.make_async_copy(refs[n], target, sems.at[n]))
            for copy in copies:
                copy.start()
            for copy in copies:
                copy.wait()

        return pl.pallas_call(
            body,
            grid_spec=pltpu.PrefetchScalarGridSpec(
                num_scalar_prefetch=1,
                grid=(),
                in_specs=[pl.BlockSpec(memory_space=pl.ANY)] * 10,
                out_specs=pl.BlockSpec(memory_space=pl.ANY),
                scratch_shapes=[pltpu.SemaphoreType.DMA((10,))],
            ),
            out_shape=jax.ShapeDtypeStruct(shape, own.dtype),
            name="assemble",
        )(at, *parts, *others)


def pad_blocks(values, axis, blocks, padded):
    shape = values.shape
    size = shape[axis] // blocks
    values = values.reshape(shape[:axis] + (blocks, size) + shape[axis + 1 :])
    pads = [(0, 0)] * values.ndim
    pads[axis + 1] = (0, padded - size)
    values = jnp.pad(values, pads)
    return values.reshape(shape[:axis] + (blocks * padded,) + shape[axis + 1 :])


def cut_blocks(values, axis, blocks, size):
    shape = values.shape
    padded = shape[axis] // blocks
    values = values.reshape(shape[:axis] + (blocks, padded) + shape[axis + 1 :])
    values = lax.slice_in_dim(values, 0, size, axis=axis + 1)
    return values.reshape(shape[:axis] + (blocks * size,) + shape[axis + 1 :])


def tiles_of(size):
    return -(-size // 128)


def exchange(parts, owner, devices):
    padded = [jnp.pad(part, ((0, 0), (0, -part.shape[1] % 128))) for part in parts]
    joined = jnp.concatenate(padded, axis=1).astype(BF)
    rank, total = joined.shape
    width = -(-total // (devices * 128)) * 128
    joined = jnp.pad(joined, ((0, 0), (0, devices * width - total)))
    pieces = joined.reshape(rank, devices, width).transpose(1, 0, 2)
    pieces = lax.all_to_all(pieces, ("dp", "seq"), split_axis=0, concat_axis=0, tiled=True)
    sums = dot(owner, pieces.reshape(devices, rank * width), ((0,), (0,))).astype(BF)
    return sums.reshape(-1, width)


def write_grads(early, late, width, hidden_size):
    columns = early.shape[1]

    def body(early_ref, late_ref, down_a, up_a, down_1, up_1, down_2, up_2):
        def spread(ref, start, target, size, turned):
            per = ref.shape[2] // 128
            for n in range(tiles_of(size)):
                device, tile = divmod(start + n, per)
                count = min(128, size - n * 128)
                block = ref[device, :, tile * 128 : (tile + 1) * 128].astype(F32)
                if turned:
                    block = jnp.transpose(block)
                    target[n * 128 : n * 128 + count, :] = block[:count, :]
                else:
                    target[:, n * 128 : n * 128 + count] = block[:, :count]
            return start + tiles_of(size)

        at = spread(early_ref, 0, down_2, hidden_size, True)
        at = spread(early_ref, at, up_1, hidden_size, False)
        at = spread(early_ref, at, up_2, width, False)
        at = spread(early_ref, at, down_1, width, True)
        at = spread(early_ref, at, down_a.at[3], width, True)
        spread(early_ref, at, up_a.at[3], width, False)
        at = 0
        for index in range(3):
            at = spread(late_ref, at, down_a.at[index], width, True)
            at = spread(late_ref, at, up_a.at[index], width, False)

    shapes = (
        (4, width, columns),
        (4, columns, width),
        (width, columns),
        (columns, hidden_size),
        (hidden_size, columns),
        (columns, width),
    )
    return pl.pallas_call(
        body,
        out_shape=[jax.ShapeDtypeStruct(shape, F32) for shape in shapes],
        name="write_grads",
    )(early, late)


def local(
    dp_size,
    seq_size,
    tokens,
    out_grad,
    image_count,
    adapter_id,
    key_live,
    w_qkv,
    w_out,
    w_fc1,
    w_fc2,
    norm_gain,
    norm_bias,
    proj_bias,
    hidden_bias,
    down_attn,
    up_attn,
    down_fc1,
    up_fc1,
    down_fc2,
    up_fc2,
):
    images, local_len, width = tokens.shape
    rows = width // seq_size
    hidden_size = hidden_bias.shape[0]
    columns = down_attn.shape[-1]
    adapters = columns // RANK
    devices = dp_size * seq_size
    place = Place(dp_size, seq_size)
    own_slot = jnp.minimum(place.slot, images - 1)
    is_live = (place.slot < image_count[0]) & (place.slot < images)
    live = is_live.astype(F32)
    adapter = lax.dynamic_index_in_dim(adapter_id, own_slot, keepdims=False)
    key_mask = lax.dynamic_index_in_dim(key_live, own_slot, keepdims=False)
    owner = jnp.where(is_live & (jnp.arange(adapters) == adapter), 1.0, 0.0)
    owner = lax.all_gather(owner.astype(BF)[None], ("dp", "seq"), axis=0, tiled=True)

    flat = place.to_image(tokens).astype(F32)

    part8 = place.dp % 8
    core = part8 % 2
    plane = part8 // 2
    half = rows // 2
    quarter = rows // 4
    piece = jnp.concatenate(
        [
            lax.dynamic_slice(w_qkv, (core * half, 0, 0), (half, 3, width)),
            lax.dynamic_slice(w_out, (core * half, 0), (half, width))[:, None, :],
        ],
        axis=1,
    )
    piece = lax.dynamic_slice(piece, (0, plane, 0), (half, 1, width)).reshape(half, width)
    attn_own = place.gather_own(piece)
    shard = hidden_size // seq_size
    padded = -(-shard // 64) * 64
    hidden_pad = padded * seq_size
    piece = lax.dynamic_slice(w_fc1, (plane * quarter, 0), (quarter, hidden_size))
    piece = pad_blocks(piece, 1, seq_size, padded)
    piece = lax.dynamic_slice(piece, (0, core * (hidden_pad // 2)), (quarter, hidden_pad // 2))
    attn_own, piece = lax.optimization_barrier((attn_own, piece))
    fc1_own = place.gather_own(piece)
    fc2 = jnp.pad(w_fc2, ((0, padded - shard), (0, 0)))
    piece = lax.dynamic_slice(fc2, (part8 * (padded // 8), 0), (padded // 8, width))
    fc1_own, piece = lax.optimization_barrier((fc1_own, piece))
    fc2_own = place.gather_own(piece)

    attn_full = place.gather_rest(
        attn_own,
        (4, seq_size, 2, half, width),
        lambda part, at: (part // 2, at, part % 2),
    ).reshape(4, width, width)
    fc1_full = place.gather_rest(
        fc1_own,
        (2, seq_size, 4, quarter, hidden_pad // 2),
        lambda part, at: (part % 2, at, part // 2),
    ).reshape(2, width, hidden_pad // 2)
    fc2_full = place.gather_rest(
        fc2_own, (seq_size, 8, padded // 8, width), lambda part, at: (at, part)
    ).reshape(2, hidden_pad // 2, width)

    def take(values, axis):
        return lax.dynamic_slice_in_dim(values, adapter * RANK, RANK, axis=axis)

    down_a = take(down_attn, 2)
    up_a = take(up_attn, 1)
    down_1 = take(down_fc1, 1)
    up_1 = pad_blocks(take(up_fc1, 0), 1, seq_size, padded)
    down_2 = pad_blocks(take(down_fc2, 1), 0, seq_size, padded)
    up_2 = take(up_fc2, 0)
    bias_1 = pad_blocks(hidden_bias, 0, seq_size, padded)

    full_len = flat.shape[0]
    heads = width // HD

    flat, owner = lax.optimization_barrier((flat, owner))
    normed = layer_norm(flat, norm_gain[0], norm_bias[0]).astype(BF)
    normed, out_grad = lax.optimization_barrier((normed, out_grad))
    top_grad = place.to_image(out_grad).astype(F32) * live
    rank_parts = []
    projected = []
    for index in range(3):
        rank_part = product(normed, down_a[index]).astype(BF)
        rank_parts.append(rank_part)
        projected.append(product(normed, attn_full[index]) + product(rank_part, up_a[index]))
    queries = (projected[0] + proj_bias[0]).astype(BF)
    key_rows = projected[1].astype(BF)
    value_rows = (projected[2] + proj_bias[1]).astype(BF)

    groups = 4

    def split_heads(values):
        values = values.reshape(full_len, groups, heads // groups, HD)
        return values.transpose(1, 0, 2, 3)

    def join_heads(values):
        return values.transpose(1, 0, 2, 3).reshape(full_len, width)

    split_q, split_k, split_v = split_heads(queries), split_heads(key_rows), split_heads(value_rows)
    masks = jnp.broadcast_to(key_mask[None], (groups, full_len))
    attended, log_total = lax.map(attend_heads, (split_q, split_k, split_v, masks))
    merged = join_heads(attended).astype(BF)
    rank_out = product(merged, down_a[3]).astype(BF)
    resid = flat + product(merged, attn_full[3]) + product(rank_out, up_a[3]) + proj_bias[2]
    normed_two = layer_norm(resid, norm_gain[1], norm_bias[1]).astype(BF)
    rank_one = product(normed_two, down_1).astype(BF)
    two_grad = top_grad.astype(BF)
    inner_two = product_back(two_grad, up_2).astype(BF)
    branch_two = proj_bias[3]
    rank_two = 0.0
    inner_one = 0.0
    normed_two_grad = 0.0
    down_2_halves = []
    up_1_halves = []
    side = hidden_pad // 2
    for index in range(2):
        at = slice(index * side, (index + 1) * side)
        hidden = product(normed_two, fc1_full[index]) + product(rank_one, up_1[:, at]) + bias_1[at]
        activated = gelu_tanh(hidden).astype(BF)
        rank_two = rank_two + product(activated, down_2[at])
        branch_two = branch_two + product(activated, fc2_full[index])
        down_2_halves.append(outer_sum(inner_two, activated))
        act_grad = product_back(two_grad, fc2_full[index]) + product_back(inner_two, down_2[at])
        hidden_grad = jax.vjp(gelu_tanh, hidden)[1](act_grad)[0].astype(BF)
        inner_one = inner_one + product_back(hidden_grad, up_1[:, at])
        up_1_halves.append(outer_sum(rank_one, hidden_grad))
        normed_two_grad = normed_two_grad + product_back(hidden_grad, fc1_full[index])
    rank_two = rank_two.astype(BF)
    branch_two = branch_two + product(rank_two, up_2)
    result = ((resid + branch_two) * live).astype(BF)
    up_2_grad = outer_sum(rank_two, two_grad)
    down_2_grad = cut_blocks(jnp.concatenate(down_2_halves, axis=1), 1, seq_size, shard)
    inner_one = inner_one.astype(BF)
    up_1_grad = cut_blocks(jnp.concatenate(up_1_halves, axis=1), 1, seq_size, shard)
    down_1_grad = outer_sum(inner_one, normed_two)
    normed_two_grad = normed_two_grad + product_back(inner_one, down_1)
    resid_grad = top_grad + norm_back(resid, norm_gain[1], norm_bias[1], normed_two_grad)
    branch_grad = resid_grad.astype(BF)
    inner_o = product_back(branch_grad, up_a[3]).astype(BF)
    up_o_grad = outer_sum(rank_out, branch_grad)
    down_o_grad = outer_sum(inner_o, merged)
    merged_grad = product_back(branch_grad, attn_full[3]) + product_back(inner_o, down_a[3])
    merged_grad = merged_grad.astype(BF)
    early = exchange(
        [down_2_grad, up_1_grad, up_2_grad, down_1_grad, down_o_grad, up_o_grad], owner, devices
    )
    early, merged_grad, result = lax.optimization_barrier((early, merged_grad, result))
    early = lax.all_gather(early, ("dp", "seq"), axis=0)
    result = place.to_tokens(result, images)

    grad_q, grad_k, grad_v = lax.map(
        attend_back, (split_q, split_k, split_v, masks, log_total, split_heads(merged_grad))
    )
    proj_grads = (join_heads(grad_q), join_heads(grad_k), join_heads(grad_v))
    normed_grad = 0.0
    late_parts = []
    for index in range(3):
        inner = product_back(proj_grads[index], up_a[index]).astype(BF)
        late_parts.append(outer_sum(inner, normed))
        late_parts.append(outer_sum(rank_parts[index], proj_grads[index]))
        normed_grad = (
            normed_grad
            + product_back(proj_grads[index], attn_full[index])
            + product_back(inner, down_a[index])
        )
    late = exchange(late_parts, owner, devices)
    late = lax.all_gather(late, ("dp", "seq"), axis=0)
    input_grad = resid_grad + norm_back(flat, norm_gain[0], norm_bias[0], normed_grad)
    input_grad = place.to_tokens(input_grad.astype(BF), images).astype(F32)
    return (result, input_grad, *write_grads(early, late, width, hidden_size))


def solution(mesh):
    in_specs = (
        P("dp", "seq", None),
        P("dp", "seq", None),
        P("dp"),
        P("dp"),
        P("dp", None),
        P("seq", None, None),
        P("seq", None),
        P("seq", None),
        P("seq", None),
        P(),
        P(),
        P(),
        P(),
        P(),
        P(),
        P(),
        P(),
        P(),
        P(),
    )
    out_specs = (P("dp", "seq", None), P("dp", "seq", None), P(), P(), P(), P(), P(), P())

    def run(*args):
        return local(mesh.shape["dp"], mesh.shape["seq"], *args)

    return jax.shard_map(run, mesh=mesh, in_specs=in_specs, out_specs=out_specs, check_vma=False)
```

```python
import jax
import jax.numpy as jnp
from jax import lax
from jax.experimental import pallas as pl
from jax.experimental.pallas import tpu as pltpu
from jax.sharding import PartitionSpec as P

HD = 72
RANK = 16
BF = jnp.bfloat16
F32 = jnp.float32

norm_eps = 1e-06


def dot(left, right, dims):
    return lax.dot_general(left, right, (dims, ((), ())), preferred_element_type=F32)


def product(left, right):
    return dot(left, right, ((1,), (0,)))


def product_back(grad, weight):
    return dot(grad, weight, ((1,), (1,)))


def outer_sum(left, right):
    return dot(left, right, ((0,), (0,)))


def layer_norm(values, gain, shift):
    average = jnp.mean(values, axis=-1, keepdims=True)
    centred = values - average
    variance = jnp.mean(centred * centred, axis=-1, keepdims=True)
    return centred * lax.rsqrt(variance + norm_eps) * gain + shift


def norm_back(values, gain, shift, grad):

    def local_norm(inner_values):
        return layer_norm(inner_values, gain, shift)

    return jax.vjp(local_norm, values)[1](grad)[0]


def gelu_tanh(values):
    return jax.nn.gelu(values, approximate=True)


def attend_heads(operands):
    queries, key_rows, value_rows, key_mask = operands
    scores = jnp.einsum(
        "qhd,khd->hqk", queries, key_rows, preferred_element_type=F32
    ) * HD ** (-0.5)
    scores = jnp.where(key_mask[None, None, :] > 0, scores, -1e30)
    row_top = jnp.max(scores, axis=-1, keepdims=True)
    exponent = jnp.exp(scores - row_top)
    row_total = jnp.sum(exponent, axis=-1, keepdims=True)
    attn_probs = (exponent / row_total).astype(BF)
    output = jnp.einsum("hqk,khd->qhd", attn_probs, value_rows, preferred_element_type=F32)
    return (output, (row_top + jnp.log(row_total))[:, :, 0])


def attend_back(operands):
    queries, key_rows, value_rows, key_mask, log_total, grad_out = operands
    scores = jnp.einsum(
        "qhd,khd->hqk", queries, key_rows, preferred_element_type=F32
    ) * HD ** (-0.5)
    scores = jnp.where(key_mask[None, None, :] > 0, scores, -1e30)
    attn_probs = jnp.exp(scores - log_total[:, :, None])
    grad_values = jnp.einsum(
        "hqk,qhd->khd", attn_probs.astype(BF), grad_out, preferred_element_type=F32
    )
    grad_probs = jnp.einsum("qhd,khd->hqk", grad_out, value_rows, preferred_element_type=F32)
    row_dot = jnp.sum(attn_probs * grad_probs, axis=-1, keepdims=True)
    grad_scores = (attn_probs * (grad_probs - row_dot)).astype(BF)
    grad_queries = jnp.einsum(
        "hqk,khd->qhd", grad_scores, key_rows, preferred_element_type=F32
    ) * HD ** (-0.5)
    grad_keys = jnp.einsum(
        "hqk,qhd->khd", grad_scores, queries, preferred_element_type=F32
    ) * HD ** (-0.5)
    return (grad_queries.astype(BF), grad_keys.astype(BF), grad_values.astype(BF))


class Place:
    def __init__(self, dp_size, seq_size):
        self.dp_size = dp_size
        self.seq_size = seq_size
        self.dp = lax.axis_index("dp")
        self.seq = lax.axis_index("seq")
        self.slot = self.image_of(self.dp, self.seq)

    def image_of(self, dp, seq):
        last = self.seq_size - 1
        if isinstance(dp, int):
            return last - seq if dp % 2 else seq
        return jnp.where(dp % 2 == 1, last - seq, seq)

    def flip(self, values, bit):
        pairs = [(n, n ^ bit) for n in range(self.dp_size)]
        return lax.ppermute(values, "dp", pairs)

    def to_image(self, values):
        images, length, width = values.shape
        size = self.seq_size
        full = jnp.zeros((size, length, width), values.dtype)
        for step in range(size):
            slot = jnp.minimum(self.image_of(self.dp, (self.seq + step) % size), images - 1)
            part = lax.dynamic_slice(values, (slot, 0, 0), (1, length, width))
            if step:
                pairs = []
                for dp in range(self.dp_size):
                    for seq in range(size):
                        target = (seq + step) % size
                        if self.image_of(dp, target) < images:
                            pairs.append((dp * size + seq, dp * size + target))
                part = lax.ppermute(part, ("dp", "seq"), pairs)
            full = lax.dynamic_update_slice(full, part, ((self.seq - step) % size, 0, 0))
        return full.reshape(size * length, width)

    def to_tokens(self, values, images):
        size = self.seq_size
        length = values.shape[0] // size
        width = values.shape[1]
        blocks = values.reshape(size, length, width)
        full = jnp.zeros((size, length, width), values.dtype)
        for step in range(size):
            part = lax.dynamic_slice(
                blocks, ((self.seq + step) % size, 0, 0), (1, length, width)
            )
            if step:
                pairs = []
                for dp in range(self.dp_size):
                    for seq in range(size):
                        if self.image_of(dp, seq) < images:
                            pairs.append((dp * size + seq, dp * size + (seq + step) % size))
                part = lax.ppermute(part, ("dp", "seq"), pairs)
            slot = self.image_of(self.dp, (self.seq - step) % size)
            full = lax.dynamic_update_slice(full, part, (slot, 0, 0))
        return full[:images]

    def gather_own(self, piece):
        return lax.all_gather(piece, "seq", axis=0)

    def gather_rest(self, own, shapes, index):
        half = self.seq_size // 2
        over_x = self.flip(own, 2)
        over_y = self.flip(own, 4)
        corner_a = self.flip(over_x[:half], 4)
        corner_b = self.flip(over_y[half:], 2)
        parts = [own, over_x, over_y, corner_a, corner_b]
        masks = [0, 2, 4, 6, 6]
        starts = [0, 0, 0, 0, half]
        others = [self.flip(part, 1) for part in parts]
        at = (self.dp % 8).astype(jnp.int32).reshape(1)

        def body(at_ref, *refs):
            outs, sems = refs[10:-1], refs[-1]
            waits = []
            for n in range(10):
                part = at_ref[0] ^ (masks[n % 5] ^ (n // 5))
                rows = pl.ds(starts[n % 5], parts[n % 5].shape[0])
                which, place = index(part, rows)
                copies = [pltpu.make_async_copy(refs[n], out.at[place], sems.at[n]) for out in outs]
                if len(outs) == 1:
                    copies[0].start()
                else:
                    for m, copy in enumerate(copies):
                        pl.when(which == m)(copy.start)
                waits.append(copies[0])
            for copy in waits:
                copy.wait()

        return pl.pallas_call(
            body,
            grid_spec=pltpu.PrefetchScalarGridSpec(
                num_scalar_prefetch=1,
                grid=(),
                in_specs=[pl.BlockSpec(memory_space=pltpu.VMEM)] * 10,
                out_specs=[pl.BlockSpec(memory_space=pl.ANY)] * len(shapes),
                scratch_shapes=[pltpu.SemaphoreType.DMA((10,))],
            ),
            out_shape=[jax.ShapeDtypeStruct(shape, own.dtype) for shape in shapes],
            name="assemble",
        )(at, *parts, *others)

    def gather_all(self, values):
        rows, width = values.shape
        if self.dp_size != 8:
            return lax.all_gather(values, ("dp", "seq"), axis=0)
        full = self.gather_rest(
            self.gather_own(values),
            [(8, self.seq_size, rows, width)],
            lambda part, at: (0, (part, at)),
        )
        return full[0].reshape(8 * self.seq_size, rows, width)


def pad_blocks(values, axis, blocks, padded):
    shape = values.shape
    size = shape[axis] // blocks
    values = values.reshape(shape[:axis] + (blocks, size) + shape[axis + 1 :])
    pads = [(0, 0)] * values.ndim
    pads[axis + 1] = (0, padded - size)
    values = jnp.pad(values, pads)
    return values.reshape(shape[:axis] + (blocks * padded,) + shape[axis + 1 :])


def cut_blocks(values, axis, blocks, size):
    shape = values.shape
    padded = shape[axis] // blocks
    values = values.reshape(shape[:axis] + (blocks, padded) + shape[axis + 1 :])
    values = lax.slice_in_dim(values, 0, size, axis=axis + 1)
    return values.reshape(shape[:axis] + (blocks * size,) + shape[axis + 1 :])


def tiles_of(size):
    return -(-size // 128)


def exchange(parts, devices, owner=None, info=None):
    padded = [jnp.pad(part, ((0, 0), (0, -part.shape[1] % 128))) for part in parts]
    joined = jnp.concatenate(padded, axis=1).astype(BF)
    rank, total = joined.shape
    width = -(-total // (devices * 128)) * 128
    joined = jnp.pad(joined, ((0, 0), (0, devices * width - total)))
    pieces = joined.reshape(rank, devices, width).transpose(1, 0, 2)
    if owner is None:
        tile = jnp.pad(info, (0, 128 - info.shape[0])).astype(BF)
        tile = jnp.broadcast_to(tile, (devices, rank, 128))
        pieces = jnp.concatenate([pieces, tile], axis=2)
    pieces = lax.all_to_all(pieces, ("dp", "seq"), split_axis=0, concat_axis=0, tiled=True)
    if owner is None:
        owner = pieces[:, 0, width : width + info.shape[0]]
    sums = dot(owner, pieces[:, :, :width].reshape(devices, rank * width), ((0,), (0,)))
    return sums.astype(BF).reshape(-1, width), owner


def write_grads(early, late, width, hidden_size):
    columns = early.shape[1]

    def body(early_ref, late_ref, down_a, up_a, down_1, up_1, down_2, up_2):
        def spread(ref, start, target, size, turned):
            per = ref.shape[2] // 128
            for n in range(tiles_of(size)):
                device, tile = divmod(start + n, per)
                count = min(128, size - n * 128)
                block = ref[device, :, tile * 128 : (tile + 1) * 128].astype(F32)
                if turned:
                    block = jnp.transpose(block)
                    target[n * 128 : n * 128 + count, :] = block[:count, :]
                else:
                    target[:, n * 128 : n * 128 + count] = block[:, :count]
            return start + tiles_of(size)

        at = spread(early_ref, 0, down_2, hidden_size, True)
        at = spread(early_ref, at, up_1, hidden_size, False)
        at = spread(early_ref, at, up_2, width, False)
        at = spread(early_ref, at, down_1, width, True)
        at = spread(early_ref, at, down_a.at[3], width, True)
        spread(early_ref, at, up_a.at[3], width, False)
        at = 0
        for index in range(3):
            at = spread(late_ref, at, down_a.at[index], width, True)
            at = spread(late_ref, at, up_a.at[index], width, False)

    shapes = (
        (4, width, columns),
        (4, columns, width),
        (width, columns),
        (columns, hidden_size),
        (hidden_size, columns),
        (columns, width),
    )
    return pl.pallas_call(
        body,
        out_shape=[jax.ShapeDtypeStruct(shape, F32) for shape in shapes],
        name="write_grads",
    )(early, late)


def local(
    dp_size,
    seq_size,
    tokens,
    out_grad,
    image_count,
    adapter_id,
    key_live,
    w_qkv,
    w_out,
    w_fc1,
    w_fc2,
    norm_gain,
    norm_bias,
    proj_bias,
    hidden_bias,
    down_attn,
    up_attn,
    down_fc1,
    up_fc1,
    down_fc2,
    up_fc2,
):
    images, local_len, width = tokens.shape
    rows = width // seq_size
    hidden_size = hidden_bias.shape[0]
    columns = down_attn.shape[-1]
    adapters = columns // RANK
    devices = dp_size * seq_size
    place = Place(dp_size, seq_size)
    own_slot = jnp.minimum(place.slot, images - 1)
    is_live = (place.slot < image_count[0]) & (place.slot < images)
    live = is_live.astype(F32)
    adapter = lax.dynamic_index_in_dim(adapter_id, own_slot, keepdims=False)
    key_mask = lax.dynamic_index_in_dim(key_live, own_slot, keepdims=False)
    info = jnp.where(is_live & (jnp.arange(adapters) == adapter), 1.0, 0.0)

    flat = place.to_image(tokens).astype(F32)

    part8 = place.dp % 8
    core = part8 % 2
    plane = part8 // 2
    half = rows // 2
    quarter = rows // 4
    piece = jnp.concatenate(
        [
            lax.dynamic_slice(w_qkv, (core * half, 0, 0), (half, 3, width)),
            lax.dynamic_slice(w_out, (core * half, 0), (half, width))[:, None, :],
        ],
        axis=1,
    )
    piece = lax.dynamic_slice(piece, (0, plane, 0), (half, 1, width)).reshape(half, width)
    attn_own = place.gather_own(piece)
    shard = hidden_size // seq_size
    padded = -(-shard // 64) * 64
    hidden_pad = padded * seq_size
    piece = lax.dynamic_slice(w_fc1, (plane * quarter, 0), (quarter, hidden_size))
    piece = pad_blocks(piece, 1, seq_size, padded)
    piece = lax.dynamic_slice(piece, (0, core * (hidden_pad // 2)), (quarter, hidden_pad // 2))
    attn_own, piece = lax.optimization_barrier((attn_own, piece))
    fc1_own = place.gather_own(piece)
    fc2 = jnp.pad(w_fc2, ((0, padded - shard), (0, 0)))
    piece = lax.dynamic_slice(fc2, (part8 * (padded // 8), 0), (padded // 8, width))
    fc1_own, piece = lax.optimization_barrier((fc1_own, piece))
    fc2_own = place.gather_own(piece)

    attn_full = place.gather_rest(
        attn_own,
        [(seq_size, 2, half, width)] * 4,
        lambda part, at: (part // 2, (at, part % 2)),
    )
    attn_full = [values.reshape(width, width) for values in attn_full]
    side = hidden_pad // 2
    fc1_full = place.gather_rest(
        fc1_own,
        [(seq_size, 4, quarter, side)] * 2,
        lambda part, at: (part % 2, (at, part // 2)),
    )
    fc1_full = [values.reshape(width, side) for values in fc1_full]
    fc2_full = place.gather_rest(
        fc2_own,
        [(seq_size, 8, padded // 8, width)],
        lambda part, at: (0, (at, part)),
    )[0].reshape(2, side, width)

    def take(values, axis):
        return lax.dynamic_slice_in_dim(values, adapter * RANK, RANK, axis=axis)

    down_a = take(down_attn, 2)
    up_a = take(up_attn, 1)
    down_1 = take(down_fc1, 1)
    up_1 = pad_blocks(take(up_fc1, 0), 1, seq_size, padded)
    down_2 = pad_blocks(take(down_fc2, 1), 0, seq_size, padded)
    up_2 = take(up_fc2, 0)
    bias_1 = pad_blocks(hidden_bias, 0, seq_size, padded)

    full_len = flat.shape[0]
    heads = width // HD

    normed = layer_norm(flat, norm_gain[0], norm_bias[0]).astype(BF)
    normed, out_grad = lax.optimization_barrier((normed, out_grad))
    top_grad = place.to_image(out_grad).astype(F32) * live
    rank_parts = []
    projected = []
    for index in range(3):
        rank_part = product(normed, down_a[index]).astype(BF)
        rank_parts.append(rank_part)
        projected.append(product(normed, attn_full[index]) + product(rank_part, up_a[index]))
    queries = (projected[0] + proj_bias[0]).astype(BF)
    key_rows = projected[1].astype(BF)
    value_rows = (projected[2] + proj_bias[1]).astype(BF)

    groups = 4

    def split_heads(values):
        values = values.reshape(full_len, groups, heads // groups, HD)
        return values.transpose(1, 0, 2, 3)

    def join_heads(values):
        return values.transpose(1, 0, 2, 3).reshape(full_len, width)

    split_q, split_k, split_v = split_heads(queries), split_heads(key_rows), split_heads(value_rows)
    masks = jnp.broadcast_to(key_mask[None], (groups, full_len))
    attended, log_total = lax.map(attend_heads, (split_q, split_k, split_v, masks))
    merged = join_heads(attended).astype(BF)
    rank_out = product(merged, down_a[3]).astype(BF)
    resid = flat + product(merged, attn_full[3]) + product(rank_out, up_a[3]) + proj_bias[2]
    normed_two = layer_norm(resid, norm_gain[1], norm_bias[1]).astype(BF)
    rank_one = product(normed_two, down_1).astype(BF)
    two_grad = top_grad.astype(BF)
    inner_two = product_back(two_grad, up_2).astype(BF)
    branch_two = proj_bias[3]
    rank_two = 0.0
    inner_one = 0.0
    normed_two_grad = 0.0
    down_2_halves = []
    up_1_halves = []
    for index in range(2):
        at = slice(index * side, (index + 1) * side)
        hidden = product(normed_two, fc1_full[index]) + product(rank_one, up_1[:, at]) + bias_1[at]
        activated = gelu_tanh(hidden).astype(BF)
        rank_two = rank_two + product(activated, down_2[at])
        branch_two = branch_two + product(activated, fc2_full[index])
        down_2_halves.append(outer_sum(inner_two, activated))
        act_grad = product_back(two_grad, fc2_full[index]) + product_back(inner_two, down_2[at])
        hidden_grad = jax.vjp(gelu_tanh, hidden)[1](act_grad)[0].astype(BF)
        inner_one = inner_one + product_back(hidden_grad, up_1[:, at])
        up_1_halves.append(outer_sum(rank_one, hidden_grad))
        normed_two_grad = normed_two_grad + product_back(hidden_grad, fc1_full[index])
    rank_two = rank_two.astype(BF)
    branch_two = branch_two + product(rank_two, up_2)
    result = ((resid + branch_two) * live).astype(BF)
    up_2_grad = outer_sum(rank_two, two_grad)
    down_2_grad = cut_blocks(jnp.concatenate(down_2_halves, axis=1), 1, seq_size, shard)
    inner_one = inner_one.astype(BF)
    up_1_grad = cut_blocks(jnp.concatenate(up_1_halves, axis=1), 1, seq_size, shard)
    down_1_grad = outer_sum(inner_one, normed_two)
    normed_two_grad = normed_two_grad + product_back(inner_one, down_1)
    resid_grad = top_grad + norm_back(resid, norm_gain[1], norm_bias[1], normed_two_grad)
    branch_grad = resid_grad.astype(BF)
    inner_o = product_back(branch_grad, up_a[3]).astype(BF)
    up_o_grad = outer_sum(rank_out, branch_grad)
    down_o_grad = outer_sum(inner_o, merged)
    merged_grad = product_back(branch_grad, attn_full[3]) + product_back(inner_o, down_a[3])
    merged_grad = merged_grad.astype(BF)
    early, owner = exchange(
        [down_2_grad, up_1_grad, up_2_grad, down_1_grad, down_o_grad, up_o_grad], devices, info=info
    )
    early, merged_grad, result = lax.optimization_barrier((early, merged_grad, result))
    early = place.gather_all(early)
    result = place.to_tokens(result, images)

    grad_q, grad_k, grad_v = lax.map(
        attend_back, (split_q, split_k, split_v, masks, log_total, split_heads(merged_grad))
    )
    proj_grads = (join_heads(grad_q), join_heads(grad_k), join_heads(grad_v))
    normed_grad = 0.0
    late_parts = []
    for index in range(3):
        inner = product_back(proj_grads[index], up_a[index]).astype(BF)
        late_parts.append(outer_sum(inner, normed))
        late_parts.append(outer_sum(rank_parts[index], proj_grads[index]))
        normed_grad = (
            normed_grad
            + product_back(proj_grads[index], attn_full[index])
            + product_back(inner, down_a[index])
        )
    late, _ = exchange(late_parts, devices, owner=owner)
    late = place.gather_all(late)
    input_grad = resid_grad + norm_back(flat, norm_gain[0], norm_bias[0], normed_grad)
    input_grad = place.to_tokens(input_grad.astype(BF), images).astype(F32)
    return (result, input_grad, *write_grads(early, late, width, hidden_size))


def solution(mesh):
    in_specs = (
        P("dp", "seq", None),
        P("dp", "seq", None),
        P("dp"),
        P("dp"),
        P("dp", None),
        P("seq", None, None),
        P("seq", None),
        P("seq", None),
        P("seq", None),
        P(),
        P(),
        P(),
        P(),
        P(),
        P(),
        P(),
        P(),
        P(),
        P(),
    )
    out_specs = (P("dp", "seq", None), P("dp", "seq", None), P(), P(), P(), P(), P(), P())

    def run(*args):
        return local(mesh.shape["dp"], mesh.shape["seq"], *args)

    return jax.shard_map(run, mesh=mesh, in_specs=in_specs, out_specs=out_specs, check_vma=False)
```

```python
import jax
import jax.numpy as jnp
from jax import lax
from jax.experimental import pallas as pl
from jax.experimental.pallas import tpu as pltpu
from jax.sharding import PartitionSpec as P

HD = 72
RANK = 16
BF = jnp.bfloat16
F32 = jnp.float32

norm_eps = 1e-06


def dot(left, right, dims):
    return lax.dot_general(left, right, (dims, ((), ())), preferred_element_type=F32)


def product(left, right):
    return dot(left, right, ((1,), (0,)))


def product_back(grad, weight):
    return dot(grad, weight, ((1,), (1,)))


def outer_sum(left, right):
    return dot(left, right, ((0,), (0,)))


def layer_norm(values, gain, shift):
    average = jnp.mean(values, axis=-1, keepdims=True)
    centred = values - average
    variance = jnp.mean(centred * centred, axis=-1, keepdims=True)
    return centred * lax.rsqrt(variance + norm_eps) * gain + shift


def norm_back(values, gain, shift, grad):

    def local_norm(inner_values):
        return layer_norm(inner_values, gain, shift)

    return jax.vjp(local_norm, values)[1](grad)[0]


def gelu_tanh(values):
    return jax.nn.gelu(values, approximate=True)


def masked_scores(key_rows, queries, mask):
    scores = lax.dot_general(key_rows, queries, (((0,), (0,)), ((), ())), preferred_element_type=F32)
    return jnp.where(mask > 0, scores * HD ** (-0.5), -1e30)


def attend(queries, key_rows, value_rows, mask):
    width, length = queries.shape
    pairs = width // (2 * HD)

    def body(q_ref, k_ref, v_ref, mask_ref, out_ref, log_ref):
        for n in range(2):
            at = slice(n * HD, (n + 1) * HD)
            scores = masked_scores(k_ref[at, :], q_ref[at, :], mask_ref[...])
            top = jnp.max(scores, axis=0, keepdims=True)
            exponent = jnp.exp(scores - top)
            total = jnp.sum(exponent, axis=0, keepdims=True)
            probs = (exponent * (1.0 / total)).astype(BF)
            out = lax.dot_general(
                v_ref[at, :], probs, (((1,), (0,)), ((), ())), preferred_element_type=F32
            )
            out_ref[at, :] = out.astype(BF)
            log_ref[0, n : n + 1, :] = top + jnp.log(total)

    block = pl.BlockSpec((2 * HD, length), lambda n: (n, 0))
    return pl.pallas_call(
        body,
        grid=(pairs,),
        in_specs=[block, block, block, pl.BlockSpec((length, 1), lambda n: (0, 0))],
        out_specs=[block, pl.BlockSpec((1, 2, length), lambda n: (n, 0, 0))],
        out_shape=[
            jax.ShapeDtypeStruct((width, length), BF),
            jax.ShapeDtypeStruct((pairs, 2, length), F32),
        ],
        name="attend",
    )(queries, key_rows, value_rows, mask)


def attend_grads(queries, key_rows, value_rows, mask, log_total, grad_out):
    width, length = queries.shape
    pairs = width // (2 * HD)

    def body(q_ref, k_ref, v_ref, mask_ref, log_ref, grad_ref, dq_ref, dk_ref, dv_ref):
        for n in range(2):
            at = slice(n * HD, (n + 1) * HD)
            q, k, v, grad = q_ref[at, :], k_ref[at, :], v_ref[at, :], grad_ref[at, :]
            probs = jnp.exp(masked_scores(k, q, mask_ref[...]) - log_ref[0, n : n + 1, :])
            dv = lax.dot_general(
                grad, probs.astype(BF), (((1,), (1,)), ((), ())), preferred_element_type=F32
            )
            dv_ref[at, :] = dv.astype(BF)
            grad_probs = lax.dot_general(
                v, grad, (((0,), (0,)), ((), ())), preferred_element_type=F32
            )
            row_dot = jnp.sum(probs * grad_probs, axis=0, keepdims=True)
            grad_scores = (probs * (grad_probs - row_dot)).astype(BF)
            dq = lax.dot_general(
                k, grad_scores, (((1,), (0,)), ((), ())), preferred_element_type=F32
            )
            dq_ref[at, :] = (dq * HD ** (-0.5)).astype(BF)
            dk = lax.dot_general(
                q, grad_scores, (((1,), (1,)), ((), ())), preferred_element_type=F32
            )
            dk_ref[at, :] = (dk * HD ** (-0.5)).astype(BF)

    block = pl.BlockSpec((2 * HD, length), lambda n: (n, 0))
    return pl.pallas_call(
        body,
        grid=(pairs,),
        in_specs=[
            block,
            block,
            block,
            pl.BlockSpec((length, 1), lambda n: (0, 0)),
            pl.BlockSpec((1, 2, length), lambda n: (n, 0, 0)),
            block,
        ],
        out_specs=[block] * 3,
        out_shape=[jax.ShapeDtypeStruct((width, length), BF)] * 3,
        name="attend_grads",
    )(queries, key_rows, value_rows, mask, log_total, grad_out)


class Place:
    def __init__(self, dp_size, seq_size):
        self.dp_size = dp_size
        self.seq_size = seq_size
        self.dp = lax.axis_index("dp")
        self.seq = lax.axis_index("seq")
        self.slot = self.image_of(self.dp, self.seq)

    def image_of(self, dp, seq):
        last = self.seq_size - 1
        if isinstance(dp, int):
            return last - seq if dp % 2 else seq
        return jnp.where(dp % 2 == 1, last - seq, seq)

    def flip(self, values, bit):
        pairs = [(n, n ^ bit) for n in range(self.dp_size)]
        return lax.ppermute(values, "dp", pairs)

    def to_image(self, values):
        images, length, width = values.shape
        size = self.seq_size
        full = jnp.zeros((size, length, width), values.dtype)
        for step in range(size):
            slot = jnp.minimum(self.image_of(self.dp, (self.seq + step) % size), images - 1)
            part = lax.dynamic_slice(values, (slot, 0, 0), (1, length, width))
            if step:
                pairs = []
                for dp in range(self.dp_size):
                    for seq in range(size):
                        target = (seq + step) % size
                        if self.image_of(dp, target) < images:
                            pairs.append((dp * size + seq, dp * size + target))
                part = lax.ppermute(part, ("dp", "seq"), pairs)
            full = lax.dynamic_update_slice(full, part, ((self.seq - step) % size, 0, 0))
        return full.reshape(size * length, width)

    def to_tokens(self, values, images):
        size = self.seq_size
        length = values.shape[0] // size
        width = values.shape[1]
        blocks = values.reshape(size, length, width)
        full = jnp.zeros((size, length, width), values.dtype)
        for step in range(size):
            part = lax.dynamic_slice(
                blocks, ((self.seq + step) % size, 0, 0), (1, length, width)
            )
            if step:
                pairs = []
                for dp in range(self.dp_size):
                    for seq in range(size):
                        if self.image_of(dp, seq) < images:
                            pairs.append((dp * size + seq, dp * size + (seq + step) % size))
                part = lax.ppermute(part, ("dp", "seq"), pairs)
            slot = self.image_of(self.dp, (self.seq - step) % size)
            full = lax.dynamic_update_slice(full, part, (slot, 0, 0))
        return full[:images]

    def gather_own(self, piece):
        return lax.all_gather(piece, "seq", axis=0)

    def gather_rest(self, own, shapes, index):
        half = self.seq_size // 2
        over_x = self.flip(own, 2)
        over_y = self.flip(own, 4)
        corner_a = self.flip(over_x[:half], 4)
        corner_b = self.flip(over_y[half:], 2)
        parts = [own, over_x, over_y, corner_a, corner_b]
        masks = [0, 2, 4, 6, 6]
        starts = [0, 0, 0, 0, half]
        others = [self.flip(part, 1) for part in parts]
        at = (self.dp % 8).astype(jnp.int32).reshape(1)

        def body(at_ref, *refs):
            outs, sems = refs[10:-1], refs[-1]
            waits = []
            for n in range(10):
                part = at_ref[0] ^ (masks[n % 5] ^ (n // 5))
                rows = pl.ds(starts[n % 5], parts[n % 5].shape[0])
                which, place = index(part, rows)
                copies = [pltpu.make_async_copy(refs[n], out.at[place], sems.at[n]) for out in outs]
                if len(outs) == 1:
                    copies[0].start()
                else:
                    for m, copy in enumerate(copies):
                        pl.when(which == m)(copy.start)
                waits.append(copies[0])
            for copy in waits:
                copy.wait()

        return pl.pallas_call(
            body,
            grid_spec=pltpu.PrefetchScalarGridSpec(
                num_scalar_prefetch=1,
                grid=(),
                in_specs=[pl.BlockSpec(memory_space=pltpu.VMEM)] * 10,
                out_specs=[pl.BlockSpec(memory_space=pl.ANY)] * len(shapes),
                scratch_shapes=[pltpu.SemaphoreType.DMA((10,))],
            ),
            out_shape=[jax.ShapeDtypeStruct(shape, own.dtype) for shape in shapes],
            name="assemble",
        )(at, *parts, *others)

    def gather_all(self, values):
        rows, width = values.shape
        if self.dp_size != 8:
            return lax.all_gather(values, ("dp", "seq"), axis=0)
        own = jnp.zeros((self.seq_size, rows, width), values.dtype)
        for step in range(self.seq_size):
            part = values
            if step:
                pairs = [(n, (n + step) % self.seq_size) for n in range(self.seq_size)]
                part = lax.ppermute(values, "seq", pairs)
            place = ((self.seq - step) % self.seq_size, 0, 0)
            own = lax.dynamic_update_slice(own, part[None], place)
        full = self.gather_rest(
            own,
            [(8, self.seq_size, rows, width)],
            lambda part, at: (0, (part, at)),
        )
        return full[0].reshape(8 * self.seq_size, rows, width)


def pad_blocks(values, axis, blocks, padded):
    shape = values.shape
    size = shape[axis] // blocks
    values = values.reshape(shape[:axis] + (blocks, size) + shape[axis + 1 :])
    pads = [(0, 0)] * values.ndim
    pads[axis + 1] = (0, padded - size)
    values = jnp.pad(values, pads)
    return values.reshape(shape[:axis] + (blocks * padded,) + shape[axis + 1 :])


def cut_blocks(values, axis, blocks, size):
    shape = values.shape
    padded = shape[axis] // blocks
    values = values.reshape(shape[:axis] + (blocks, padded) + shape[axis + 1 :])
    values = lax.slice_in_dim(values, 0, size, axis=axis + 1)
    return values.reshape(shape[:axis] + (blocks * size,) + shape[axis + 1 :])


def tiles_of(size):
    return -(-size // 128)


def exchange(parts, devices, owner=None, info=None):
    padded = [jnp.pad(part, ((0, 0), (0, -part.shape[1] % 128))) for part in parts]
    joined = jnp.concatenate(padded, axis=1).astype(BF)
    rank, total = joined.shape
    width = -(-total // (devices * 128)) * 128
    joined = jnp.pad(joined, ((0, 0), (0, devices * width - total)))
    pieces = joined.reshape(rank, devices, width).transpose(1, 0, 2)
    if owner is None:
        tile = jnp.pad(info, (0, 128 - info.shape[0])).astype(BF)
        tile = jnp.broadcast_to(tile, (devices, rank, 128))
        pieces = jnp.concatenate([pieces, tile], axis=2)
    pieces = lax.all_to_all(pieces, ("dp", "seq"), split_axis=0, concat_axis=0, tiled=True)
    if owner is None:
        owner = pieces[:, 0, width : width + info.shape[0]]
    sums = dot(owner, pieces[:, :, :width].reshape(devices, rank * width), ((0,), (0,)))
    return sums.astype(BF).reshape(-1, width), owner


def write_grads(early, late, width, hidden_size):
    columns = early.shape[1]

    def body(early_ref, late_ref, down_a, up_a, down_1, up_1, down_2, up_2):
        def spread(ref, start, target, size, turned):
            per = ref.shape[2] // 128
            for n in range(tiles_of(size)):
                device, tile = divmod(start + n, per)
                count = min(128, size - n * 128)
                block = ref[device, :, tile * 128 : (tile + 1) * 128].astype(F32)
                if turned:
                    block = jnp.transpose(block)
                    target[n * 128 : n * 128 + count, :] = block[:count, :]
                else:
                    target[:, n * 128 : n * 128 + count] = block[:, :count]
            return start + tiles_of(size)

        at = spread(early_ref, 0, down_2, hidden_size, True)
        at = spread(early_ref, at, up_1, hidden_size, False)
        at = spread(early_ref, at, up_2, width, False)
        at = spread(early_ref, at, down_1, width, True)
        at = spread(early_ref, at, down_a.at[3], width, True)
        spread(early_ref, at, up_a.at[3], width, False)
        at = 0
        for index in range(3):
            at = spread(late_ref, at, down_a.at[index], width, True)
            at = spread(late_ref, at, up_a.at[index], width, False)

    shapes = (
        (4, width, columns),
        (4, columns, width),
        (width, columns),
        (columns, hidden_size),
        (hidden_size, columns),
        (columns, width),
    )
    return pl.pallas_call(
        body,
        out_shape=[jax.ShapeDtypeStruct(shape, F32) for shape in shapes],
        name="write_grads",
    )(early, late)


def local(
    dp_size,
    seq_size,
    tokens,
    out_grad,
    image_count,
    adapter_id,
    key_live,
    w_qkv,
    w_out,
    w_fc1,
    w_fc2,
    norm_gain,
    norm_bias,
    proj_bias,
    hidden_bias,
    down_attn,
    up_attn,
    down_fc1,
    up_fc1,
    down_fc2,
    up_fc2,
):
    images, local_len, width = tokens.shape
    rows = width // seq_size
    hidden_size = hidden_bias.shape[0]
    columns = down_attn.shape[-1]
    adapters = columns // RANK
    devices = dp_size * seq_size
    place = Place(dp_size, seq_size)
    own_slot = jnp.minimum(place.slot, images - 1)
    is_live = (place.slot < image_count[0]) & (place.slot < images)
    live = is_live.astype(F32)
    adapter = lax.dynamic_index_in_dim(adapter_id, own_slot, keepdims=False)
    key_mask = lax.dynamic_index_in_dim(key_live, own_slot, keepdims=False)
    info = jnp.where(is_live & (jnp.arange(adapters) == adapter), 1.0, 0.0)

    flat = place.to_image(tokens).astype(F32)

    part8 = place.dp % 8
    core = part8 % 2
    plane = part8 // 2
    half = rows // 2
    quarter = rows // 4
    piece = jnp.concatenate(
        [
            lax.dynamic_slice(w_qkv, (core * half, 0, 0), (half, 3, width)),
            lax.dynamic_slice(w_out, (core * half, 0), (half, width))[:, None, :],
        ],
        axis=1,
    )
    piece = lax.dynamic_slice(piece, (0, plane, 0), (half, 1, width)).reshape(half, width)
    attn_own = place.gather_own(piece)
    shard = hidden_size // seq_size
    padded = -(-shard // 64) * 64
    hidden_pad = padded * seq_size
    piece = lax.dynamic_slice(w_fc1, (plane * quarter, 0), (quarter, hidden_size))
    piece = pad_blocks(piece, 1, seq_size, padded)
    piece = lax.dynamic_slice(piece, (0, core * (hidden_pad // 2)), (quarter, hidden_pad // 2))
    attn_own, piece = lax.optimization_barrier((attn_own, piece))
    fc1_own = place.gather_own(piece)
    fc2 = jnp.pad(w_fc2, ((0, padded - shard), (0, 0)))
    piece = lax.dynamic_slice(fc2, (part8 * (padded // 8), 0), (padded // 8, width))
    fc1_own, piece = lax.optimization_barrier((fc1_own, piece))
    fc2_own = place.gather_own(piece)

    attn_full = place.gather_rest(
        attn_own,
        [(seq_size, 2, half, width)] * 4,
        lambda part, at: (part // 2, (at, part % 2)),
    )
    attn_full = [values.reshape(width, width) for values in attn_full]
    side = hidden_pad // 2
    fc1_full = place.gather_rest(
        fc1_own,
        [(seq_size, 4, quarter, side)] * 2,
        lambda part, at: (part % 2, (at, part // 2)),
    )
    fc1_full = [values.reshape(width, side) for values in fc1_full]
    fc2_full = place.gather_rest(
        fc2_own,
        [(seq_size, 8, padded // 8, width)],
        lambda part, at: (0, (at, part)),
    )[0].reshape(2, side, width)

    def take(values, axis):
        return lax.dynamic_slice_in_dim(values, adapter * RANK, RANK, axis=axis)

    down_a = take(down_attn, 2)
    up_a = take(up_attn, 1)
    down_1 = take(down_fc1, 1)
    up_1 = pad_blocks(take(up_fc1, 0), 1, seq_size, padded)
    down_2 = pad_blocks(take(down_fc2, 1), 0, seq_size, padded)
    up_2 = take(up_fc2, 0)
    bias_1 = pad_blocks(hidden_bias, 0, seq_size, padded)

    normed = layer_norm(flat, norm_gain[0], norm_bias[0]).astype(BF)
    normed, out_grad = lax.optimization_barrier((normed, out_grad))
    top_grad = place.to_image(out_grad).astype(F32) * live
    rank_parts = []
    projected = []
    for index in range(3):
        rank_part = product(normed, down_a[index]).astype(BF)
        rank_parts.append(rank_part)
        projected.append(product(normed, attn_full[index]) + product(rank_part, up_a[index]))
    queries = (projected[0] + proj_bias[0]).astype(BF)
    key_rows = projected[1].astype(BF)
    value_rows = (projected[2] + proj_bias[1]).astype(BF)

    turned = (queries.T, key_rows.T, value_rows.T, key_mask[:, None])
    attended, log_total = attend(*turned)
    merged = attended.T
    rank_out = product(merged, down_a[3]).astype(BF)
    resid = flat + product(merged, attn_full[3]) + product(rank_out, up_a[3]) + proj_bias[2]
    normed_two = layer_norm(resid, norm_gain[1], norm_bias[1]).astype(BF)
    rank_one = product(normed_two, down_1).astype(BF)
    two_grad = top_grad.astype(BF)
    inner_two = product_back(two_grad, up_2).astype(BF)
    branch_two = proj_bias[3]
    rank_two = 0.0
    inner_one = 0.0
    normed_two_grad = 0.0
    down_2_halves = []
    up_1_halves = []
    for index in range(2):
        at = slice(index * side, (index + 1) * side)
        hidden = product(normed_two, fc1_full[index]) + product(rank_one, up_1[:, at]) + bias_1[at]
        activated = gelu_tanh(hidden).astype(BF)
        rank_two = rank_two + product(activated, down_2[at])
        branch_two = branch_two + product(activated, fc2_full[index])
        down_2_halves.append(outer_sum(inner_two, activated))
        act_grad = product_back(two_grad, fc2_full[index]) + product_back(inner_two, down_2[at])
        hidden_grad = jax.vjp(gelu_tanh, hidden)[1](act_grad)[0].astype(BF)
        inner_one = inner_one + product_back(hidden_grad, up_1[:, at])
        up_1_halves.append(outer_sum(rank_one, hidden_grad))
        normed_two_grad = normed_two_grad + product_back(hidden_grad, fc1_full[index])
    rank_two = rank_two.astype(BF)
    branch_two = branch_two + product(rank_two, up_2)
    result = ((resid + branch_two) * live).astype(BF)
    up_2_grad = outer_sum(rank_two, two_grad)
    down_2_grad = cut_blocks(jnp.concatenate(down_2_halves, axis=1), 1, seq_size, shard)
    inner_one = inner_one.astype(BF)
    up_1_grad = cut_blocks(jnp.concatenate(up_1_halves, axis=1), 1, seq_size, shard)
    down_1_grad = outer_sum(inner_one, normed_two)
    normed_two_grad = normed_two_grad + product_back(inner_one, down_1)
    resid_grad = top_grad + norm_back(resid, norm_gain[1], norm_bias[1], normed_two_grad)
    branch_grad = resid_grad.astype(BF)
    inner_o = product_back(branch_grad, up_a[3]).astype(BF)
    up_o_grad = outer_sum(rank_out, branch_grad)
    down_o_grad = outer_sum(inner_o, merged)
    merged_grad = product_back(branch_grad, attn_full[3]) + product_back(inner_o, down_a[3])
    merged_grad = merged_grad.astype(BF)
    early, owner = exchange(
        [down_2_grad, up_1_grad, up_2_grad, down_1_grad, down_o_grad, up_o_grad], devices, info=info
    )
    early, merged_grad, result = lax.optimization_barrier((early, merged_grad, result))
    early = place.gather_all(early)
    result = place.to_tokens(result, images)

    proj_grads = [grad.T for grad in attend_grads(*turned, log_total, merged_grad.T)]
    normed_grad = 0.0
    late_parts = []
    for index in range(3):
        inner = product_back(proj_grads[index], up_a[index]).astype(BF)
        late_parts.append(outer_sum(inner, normed))
        late_parts.append(outer_sum(rank_parts[index], proj_grads[index]))
        normed_grad = (
            normed_grad
            + product_back(proj_grads[index], attn_full[index])
            + product_back(inner, down_a[index])
        )
    late, _ = exchange(late_parts, devices, owner=owner)
    late = place.gather_all(late)
    input_grad = resid_grad + norm_back(flat, norm_gain[0], norm_bias[0], normed_grad)
    input_grad = place.to_tokens(input_grad.astype(BF), images).astype(F32)
    return (result, input_grad, *write_grads(early, late, width, hidden_size))


def solution(mesh):
    in_specs = (
        P("dp", "seq", None),
        P("dp", "seq", None),
        P("dp"),
        P("dp"),
        P("dp", None),
        P("seq", None, None),
        P("seq", None),
        P("seq", None),
        P("seq", None),
        P(),
        P(),
        P(),
        P(),
        P(),
        P(),
        P(),
        P(),
        P(),
        P(),
    )
    out_specs = (P("dp", "seq", None), P("dp", "seq", None), P(), P(), P(), P(), P(), P())

    def run(*args):
        return local(mesh.shape["dp"], mesh.shape["seq"], *args)

    return jax.shard_map(run, mesh=mesh, in_specs=in_specs, out_specs=out_specs, check_vma=False)
```

```python
import jax
import jax.numpy as jnp
from jax import lax
from jax.experimental import pallas as pl
from jax.experimental.pallas import tpu as pltpu
from jax.sharding import PartitionSpec as P

HD = 72
RANK = 16
BF = jnp.bfloat16
F32 = jnp.float32

norm_eps = 1e-06


def dot(left, right, dims):
    return lax.dot_general(left, right, (dims, ((), ())), preferred_element_type=F32)


def product(left, right):
    return dot(left, right, ((1,), (0,)))


def product_back(grad, weight):
    return dot(grad, weight, ((1,), (1,)))


def outer_sum(left, right):
    return dot(left, right, ((0,), (0,)))


def layer_norm(values, gain, shift):
    average = jnp.mean(values, axis=-1, keepdims=True)
    centred = values - average
    variance = jnp.mean(centred * centred, axis=-1, keepdims=True)
    return centred * lax.rsqrt(variance + norm_eps) * gain + shift


def norm_back(values, gain, shift, grad):

    def local_norm(inner_values):
        return layer_norm(inner_values, gain, shift)

    return jax.vjp(local_norm, values)[1](grad)[0]


def masked_scores(key_rows, queries, mask):
    scores = lax.dot_general(key_rows, queries, (((0,), (0,)), ((), ())), preferred_element_type=F32)
    return jnp.where(mask > 0, scores * HD ** (-0.5), -1e30)


def attend(queries, key_rows, value_rows, mask):
    width, length = queries.shape
    pairs = width // (2 * HD)

    def body(q_ref, k_ref, v_ref, mask_ref, out_ref, log_ref):
        for n in range(2):
            at = slice(n * HD, (n + 1) * HD)
            scores = masked_scores(k_ref[at, :], q_ref[at, :], mask_ref[...])
            top = jnp.max(scores, axis=0, keepdims=True)
            exponent = jnp.exp(scores - top)
            total = jnp.sum(exponent, axis=0, keepdims=True)
            probs = (exponent * (1.0 / total)).astype(BF)
            out = lax.dot_general(
                v_ref[at, :], probs, (((1,), (0,)), ((), ())), preferred_element_type=F32
            )
            out_ref[at, :] = out.astype(BF)
            log_ref[0, n : n + 1, :] = top + jnp.log(total)

    block = pl.BlockSpec((2 * HD, length), lambda n: (n, 0))
    return pl.pallas_call(
        body,
        grid=(pairs,),
        in_specs=[block, block, block, pl.BlockSpec((length, 1), lambda n: (0, 0))],
        out_specs=[block, pl.BlockSpec((1, 2, length), lambda n: (n, 0, 0))],
        out_shape=[
            jax.ShapeDtypeStruct((width, length), BF),
            jax.ShapeDtypeStruct((pairs, 2, length), F32),
        ],
        name="attend",
    )(queries, key_rows, value_rows, mask)


def attend_grads(queries, key_rows, value_rows, mask, log_total, grad_out):
    width, length = queries.shape
    pairs = width // (2 * HD)

    def body(q_ref, k_ref, v_ref, mask_ref, log_ref, grad_ref, dq_ref, dk_ref, dv_ref):
        for n in range(2):
            at = slice(n * HD, (n + 1) * HD)
            q, k, v, grad = q_ref[at, :], k_ref[at, :], v_ref[at, :], grad_ref[at, :]
            probs = jnp.exp(masked_scores(k, q, mask_ref[...]) - log_ref[0, n : n + 1, :])
            dv = lax.dot_general(
                grad, probs.astype(BF), (((1,), (1,)), ((), ())), preferred_element_type=F32
            )
            dv_ref[at, :] = dv.astype(BF)
            grad_probs = lax.dot_general(
                v, grad, (((0,), (0,)), ((), ())), preferred_element_type=F32
            )
            row_dot = jnp.sum(probs * grad_probs, axis=0, keepdims=True)
            grad_scores = (probs * (grad_probs - row_dot)).astype(BF)
            dq = lax.dot_general(
                k, grad_scores, (((1,), (0,)), ((), ())), preferred_element_type=F32
            )
            dq_ref[at, :] = (dq * HD ** (-0.5)).astype(BF)
            dk = lax.dot_general(
                q, grad_scores, (((1,), (1,)), ((), ())), preferred_element_type=F32
            )
            dk_ref[at, :] = (dk * HD ** (-0.5)).astype(BF)

    block = pl.BlockSpec((2 * HD, length), lambda n: (n, 0))
    return pl.pallas_call(
        body,
        grid=(pairs,),
        in_specs=[
            block,
            block,
            block,
            pl.BlockSpec((length, 1), lambda n: (0, 0)),
            pl.BlockSpec((1, 2, length), lambda n: (n, 0, 0)),
            block,
        ],
        out_specs=[block] * 3,
        out_shape=[jax.ShapeDtypeStruct((width, length), BF)] * 3,
        name="attend_grads",
    )(queries, key_rows, value_rows, mask, log_total, grad_out)


def run_mlp(normed, top_grad, rank_one, inner_two, weights, bias):
    first, second, up, down = weights
    length, width = normed.shape
    rank, total = up.shape
    size = 256
    steps = total // size
    scale = (2.0 / jnp.pi) ** 0.5

    def body(
        normed_ref, grad_ref, rank_ref, inner_ref, rank_t_ref, inner_t_ref,
        first_ref, second_ref, up_ref, down_ref, bias_ref,
        branch_ref, rank_two_ref, back_ref, inner_one_ref, down_grad_ref, up_grad_ref,
    ):
        first, second, up, down = first_ref[...], second_ref[...], up_ref[...], down_ref[...]
        hidden = dot(normed_ref[...], first, ((1,), (0,))) + bias_ref[...]
        hidden = hidden + dot(rank_ref[...], up, ((1,), (0,)))
        act_grad = dot(grad_ref[...], second, ((1,), (1,)))
        act_grad = act_grad + dot(inner_ref[...], down, ((1,), (0,)))
        square = hidden * hidden
        bent = jnp.tanh(scale * hidden * (1.0 + 0.044715 * square))
        side = 0.5 * (1.0 + bent)
        activated = (hidden * side).astype(BF)
        slope = side + 0.5 * hidden * (1.0 - bent * bent) * (scale * (1.0 + 0.134145 * square))
        hidden_grad = (act_grad * slope).astype(BF)
        down_grad_ref[...] = dot(inner_t_ref[...], activated, ((1,), (0,)))
        up_grad_ref[...] = dot(rank_t_ref[...], hidden_grad, ((1,), (0,)))
        sums = (
            (branch_ref, dot(activated, second, ((1,), (0,)))),
            (rank_two_ref, dot(activated, down, ((1,), (1,)))),
            (back_ref, dot(hidden_grad, first, ((1,), (1,)))),
            (inner_one_ref, dot(hidden_grad, up, ((1,), (1,)))),
        )

        @pl.when(pl.program_id(0) == 0)
        def _():
            for ref, value in sums:
                ref[...] = value

        @pl.when(pl.program_id(0) > 0)
        def _():
            for ref, value in sums:
                ref[...] += value

    def whole(rows, cols):
        return pl.BlockSpec((rows, cols), lambda n: (0, 0))

    def tile(rows):
        return pl.BlockSpec((rows, size), lambda n: (0, n))

    return pl.pallas_call(
        body,
        grid=(steps,),
        in_specs=[
            whole(length, width),
            whole(length, width),
            whole(length, rank),
            whole(length, rank),
            whole(rank, length),
            whole(rank, length),
            tile(width),
            pl.BlockSpec((size, width), lambda n: (n, 0)),
            tile(rank),
            tile(rank),
            tile(1),
        ],
        out_specs=[
            whole(length, width),
            whole(length, rank),
            whole(length, width),
            whole(length, rank),
            tile(rank),
            tile(rank),
        ],
        out_shape=[
            jax.ShapeDtypeStruct((length, width), F32),
            jax.ShapeDtypeStruct((length, rank), F32),
            jax.ShapeDtypeStruct((length, width), F32),
            jax.ShapeDtypeStruct((length, rank), F32),
            jax.ShapeDtypeStruct((rank, total), F32),
            jax.ShapeDtypeStruct((rank, total), F32),
        ],
        name="run_mlp",
    )(
        normed, top_grad, rank_one, inner_two, rank_one.T, inner_two.T,
        first, second, up, down, bias[None],
    )


class Place:
    def __init__(self, dp_size, seq_size):
        self.dp_size = dp_size
        self.seq_size = seq_size
        self.dp = lax.axis_index("dp")
        self.seq = lax.axis_index("seq")
        self.slot = self.image_of(self.dp, self.seq)

    def image_of(self, dp, seq):
        last = self.seq_size - 1
        if isinstance(dp, int):
            return last - seq if dp % 2 else seq
        return jnp.where(dp % 2 == 1, last - seq, seq)

    def flip(self, values, bit):
        pairs = [(n, n ^ bit) for n in range(self.dp_size)]
        return lax.ppermute(values, "dp", pairs)

    def to_image(self, values):
        images, length, width = values.shape
        size = self.seq_size
        full = jnp.zeros((size, length, width), values.dtype)
        for step in range(size):
            slot = jnp.minimum(self.image_of(self.dp, (self.seq + step) % size), images - 1)
            part = lax.dynamic_slice(values, (slot, 0, 0), (1, length, width))
            if step:
                pairs = []
                for dp in range(self.dp_size):
                    for seq in range(size):
                        target = (seq + step) % size
                        if self.image_of(dp, target) < images:
                            pairs.append((dp * size + seq, dp * size + target))
                part = lax.ppermute(part, ("dp", "seq"), pairs)
            full = lax.dynamic_update_slice(full, part, ((self.seq - step) % size, 0, 0))
        return full.reshape(size * length, width)

    def to_tokens(self, values, images):
        size = self.seq_size
        length = values.shape[0] // size
        width = values.shape[1]
        blocks = values.reshape(size, length, width)
        full = jnp.zeros((size, length, width), values.dtype)
        for step in range(size):
            part = lax.dynamic_slice(
                blocks, ((self.seq + step) % size, 0, 0), (1, length, width)
            )
            if step:
                pairs = []
                for dp in range(self.dp_size):
                    for seq in range(size):
                        if self.image_of(dp, seq) < images:
                            pairs.append((dp * size + seq, dp * size + (seq + step) % size))
                part = lax.ppermute(part, ("dp", "seq"), pairs)
            slot = self.image_of(self.dp, (self.seq - step) % size)
            full = lax.dynamic_update_slice(full, part, (slot, 0, 0))
        return full[:images]

    def gather_own(self, piece):
        return lax.all_gather(piece, "seq", axis=0)

    def gather_rest(self, own, shapes, index):
        half = self.seq_size // 2
        over_x = self.flip(own, 2)
        over_y = self.flip(own, 4)
        corner_a = self.flip(over_x[:half], 4)
        corner_b = self.flip(over_y[half:], 2)
        parts = [own, over_x, over_y, corner_a, corner_b]
        masks = [0, 2, 4, 6, 6]
        starts = [0, 0, 0, 0, half]
        others = [self.flip(part, 1) for part in parts]
        at = (self.dp % 8).astype(jnp.int32).reshape(1)

        def body(at_ref, *refs):
            outs, sems = refs[10:-1], refs[-1]
            waits = []
            for n in range(10):
                part = at_ref[0] ^ (masks[n % 5] ^ (n // 5))
                rows = pl.ds(starts[n % 5], parts[n % 5].shape[0])
                which, place = index(part, rows)
                copies = [pltpu.make_async_copy(refs[n], out.at[place], sems.at[n]) for out in outs]
                if len(outs) == 1:
                    copies[0].start()
                else:
                    for m, copy in enumerate(copies):
                        pl.when(which == m)(copy.start)
                waits.append(copies[0])
            for copy in waits:
                copy.wait()

        return pl.pallas_call(
            body,
            grid_spec=pltpu.PrefetchScalarGridSpec(
                num_scalar_prefetch=1,
                grid=(),
                in_specs=[pl.BlockSpec(memory_space=pltpu.VMEM)] * 10,
                out_specs=[pl.BlockSpec(memory_space=pl.ANY)] * len(shapes),
                scratch_shapes=[pltpu.SemaphoreType.DMA((10,))],
            ),
            out_shape=[jax.ShapeDtypeStruct(shape, own.dtype) for shape in shapes],
            name="assemble",
        )(at, *parts, *others)

    def gather_all(self, values):
        rows, width = values.shape
        if self.dp_size != 8:
            return lax.all_gather(values, ("dp", "seq"), axis=0)
        own = jnp.zeros((self.seq_size, rows, width), values.dtype)
        for step in range(self.seq_size):
            part = values
            if step:
                pairs = [(n, (n + step) % self.seq_size) for n in range(self.seq_size)]
                part = lax.ppermute(values, "seq", pairs)
            place = ((self.seq - step) % self.seq_size, 0, 0)
            own = lax.dynamic_update_slice(own, part[None], place)
        full = self.gather_rest(
            own,
            [(8, self.seq_size, rows, width)],
            lambda part, at: (0, (part, at)),
        )
        return full[0].reshape(8 * self.seq_size, rows, width)


def pad_blocks(values, axis, blocks, padded):
    shape = values.shape
    size = shape[axis] // blocks
    values = values.reshape(shape[:axis] + (blocks, size) + shape[axis + 1 :])
    pads = [(0, 0)] * values.ndim
    pads[axis + 1] = (0, padded - size)
    values = jnp.pad(values, pads)
    return values.reshape(shape[:axis] + (blocks * padded,) + shape[axis + 1 :])


def cut_blocks(values, axis, blocks, size):
    shape = values.shape
    padded = shape[axis] // blocks
    values = values.reshape(shape[:axis] + (blocks, padded) + shape[axis + 1 :])
    values = lax.slice_in_dim(values, 0, size, axis=axis + 1)
    return values.reshape(shape[:axis] + (blocks * size,) + shape[axis + 1 :])


def tiles_of(size):
    return -(-size // 128)


def exchange(parts, devices, owner=None, info=None):
    padded = [jnp.pad(part, ((0, 0), (0, -part.shape[1] % 128))) for part in parts]
    joined = jnp.concatenate(padded, axis=1).astype(BF)
    rank, total = joined.shape
    width = -(-total // (devices * 128)) * 128
    joined = jnp.pad(joined, ((0, 0), (0, devices * width - total)))
    pieces = joined.reshape(rank, devices, width).transpose(1, 0, 2)
    if owner is None:
        tile = jnp.pad(info, (0, 128 - info.shape[0])).astype(BF)
        tile = jnp.broadcast_to(tile, (devices, rank, 128))
        pieces = jnp.concatenate([pieces, tile], axis=2)
    pieces = lax.all_to_all(pieces, ("dp", "seq"), split_axis=0, concat_axis=0, tiled=True)
    if owner is None:
        owner = pieces[:, 0, width : width + info.shape[0]]
    sums = dot(owner, pieces[:, :, :width].reshape(devices, rank * width), ((0,), (0,)))
    return sums.astype(BF).reshape(-1, width), owner


def write_grads(early, late, width, hidden_size):
    columns = early.shape[1]

    def body(early_ref, late_ref, down_a, up_a, down_1, up_1, down_2, up_2):
        def spread(ref, start, target, size, turned):
            per = ref.shape[2] // 128
            for n in range(tiles_of(size)):
                device, tile = divmod(start + n, per)
                count = min(128, size - n * 128)
                block = ref[device, :, tile * 128 : (tile + 1) * 128].astype(F32)
                if turned:
                    block = jnp.transpose(block)
                    target[n * 128 : n * 128 + count, :] = block[:count, :]
                else:
                    target[:, n * 128 : n * 128 + count] = block[:, :count]
            return start + tiles_of(size)

        at = spread(early_ref, 0, down_2, hidden_size, True)
        at = spread(early_ref, at, up_1, hidden_size, False)
        at = spread(early_ref, at, up_2, width, False)
        at = spread(early_ref, at, down_1, width, True)
        at = spread(early_ref, at, down_a.at[3], width, True)
        spread(early_ref, at, up_a.at[3], width, False)
        at = 0
        for index in range(3):
            at = spread(late_ref, at, down_a.at[index], width, True)
            at = spread(late_ref, at, up_a.at[index], width, False)

    shapes = (
        (4, width, columns),
        (4, columns, width),
        (width, columns),
        (columns, hidden_size),
        (hidden_size, columns),
        (columns, width),
    )
    return pl.pallas_call(
        body,
        out_shape=[jax.ShapeDtypeStruct(shape, F32) for shape in shapes],
        name="write_grads",
    )(early, late)


def local(
    dp_size,
    seq_size,
    tokens,
    out_grad,
    image_count,
    adapter_id,
    key_live,
    w_qkv,
    w_out,
    w_fc1,
    w_fc2,
    norm_gain,
    norm_bias,
    proj_bias,
    hidden_bias,
    down_attn,
    up_attn,
    down_fc1,
    up_fc1,
    down_fc2,
    up_fc2,
):
    images, local_len, width = tokens.shape
    rows = width // seq_size
    hidden_size = hidden_bias.shape[0]
    columns = down_attn.shape[-1]
    adapters = columns // RANK
    devices = dp_size * seq_size
    place = Place(dp_size, seq_size)
    own_slot = jnp.minimum(place.slot, images - 1)
    is_live = (place.slot < image_count[0]) & (place.slot < images)
    live = is_live.astype(F32)
    adapter = lax.dynamic_index_in_dim(adapter_id, own_slot, keepdims=False)
    key_mask = lax.dynamic_index_in_dim(key_live, own_slot, keepdims=False)
    info = jnp.where(is_live & (jnp.arange(adapters) == adapter), 1.0, 0.0)

    flat = place.to_image(tokens).astype(F32)

    part8 = place.dp % 8
    core = part8 % 2
    plane = part8 // 2
    half = rows // 2
    quarter = rows // 4
    piece = jnp.concatenate(
        [
            lax.dynamic_slice(w_qkv, (core * half, 0, 0), (half, 3, width)),
            lax.dynamic_slice(w_out, (core * half, 0), (half, width))[:, None, :],
        ],
        axis=1,
    )
    piece = lax.dynamic_slice(piece, (0, plane, 0), (half, 1, width)).reshape(half, width)
    attn_own = place.gather_own(piece)
    shard = hidden_size // seq_size
    padded = -(-shard // 64) * 64
    hidden_pad = padded * seq_size
    piece = lax.dynamic_slice(w_fc1, (plane * quarter, 0), (quarter, hidden_size))
    piece = pad_blocks(piece, 1, seq_size, padded)
    piece = lax.dynamic_slice(piece, (0, core * (hidden_pad // 2)), (quarter, hidden_pad // 2))
    attn_own, piece = lax.optimization_barrier((attn_own, piece))
    fc1_own = place.gather_own(piece)
    fc2 = jnp.pad(w_fc2, ((0, padded - shard), (0, 0)))
    piece = lax.dynamic_slice(fc2, (part8 * (padded // 8), 0), (padded // 8, width))
    fc1_own, piece = lax.optimization_barrier((fc1_own, piece))
    fc2_own = place.gather_own(piece)

    attn_full = place.gather_rest(
        attn_own,
        [(seq_size, 2, half, width)] * 4,
        lambda part, at: (part // 2, (at, part % 2)),
    )
    attn_full = [values.reshape(width, width) for values in attn_full]
    side = hidden_pad // 2
    fc1_full = place.gather_rest(
        fc1_own,
        [(seq_size, 4, quarter, hidden_pad)],
        lambda part, at: (
            0,
            (at, part // 2, slice(None), pl.ds(pl.multiple_of(part % 2 * side, 128), side)),
        ),
    )[0].reshape(width, hidden_pad)
    fc2_full = place.gather_rest(
        fc2_own,
        [(seq_size, 8, padded // 8, width)],
        lambda part, at: (0, (at, part)),
    )[0].reshape(hidden_pad, width)

    def take(values, axis):
        return lax.dynamic_slice_in_dim(values, adapter * RANK, RANK, axis=axis)

    down_a = take(down_attn, 2)
    up_a = take(up_attn, 1)
    down_1 = take(down_fc1, 1)
    up_1 = pad_blocks(take(up_fc1, 0), 1, seq_size, padded)
    down_2 = pad_blocks(take(down_fc2, 1), 0, seq_size, padded)
    up_2 = take(up_fc2, 0)
    bias_1 = pad_blocks(hidden_bias, 0, seq_size, padded)

    normed = layer_norm(flat, norm_gain[0], norm_bias[0]).astype(BF)
    normed, out_grad = lax.optimization_barrier((normed, out_grad))
    top_grad = place.to_image(out_grad).astype(F32) * live
    rank_parts = []
    projected = []
    for index in range(3):
        rank_part = product(normed, down_a[index]).astype(BF)
        rank_parts.append(rank_part)
        projected.append(product(normed, attn_full[index]) + product(rank_part, up_a[index]))
    queries = (projected[0] + proj_bias[0]).astype(BF)
    key_rows = projected[1].astype(BF)
    value_rows = (projected[2] + proj_bias[1]).astype(BF)

    turned = (queries.T, key_rows.T, value_rows.T, key_mask[:, None])
    attended, log_total = attend(*turned)
    merged = attended.T
    rank_out = product(merged, down_a[3]).astype(BF)
    resid = flat + product(merged, attn_full[3]) + product(rank_out, up_a[3]) + proj_bias[2]
    normed_two = layer_norm(resid, norm_gain[1], norm_bias[1]).astype(BF)
    rank_one = product(normed_two, down_1).astype(BF)
    two_grad = top_grad.astype(BF)
    inner_two = product_back(two_grad, up_2).astype(BF)
    branch_two, rank_two, normed_two_grad, inner_one, down_2_grad, up_1_grad = run_mlp(
        normed_two, two_grad, rank_one, inner_two, (fc1_full, fc2_full, up_1, down_2.T), bias_1
    )
    rank_two = rank_two.astype(BF)
    branch_two = branch_two + product(rank_two, up_2) + proj_bias[3]
    result = ((resid + branch_two) * live).astype(BF)
    up_2_grad = outer_sum(rank_two, two_grad)
    down_2_grad = cut_blocks(down_2_grad, 1, seq_size, shard)
    inner_one = inner_one.astype(BF)
    up_1_grad = cut_blocks(up_1_grad, 1, seq_size, shard)
    down_1_grad = outer_sum(inner_one, normed_two)
    normed_two_grad = normed_two_grad + product_back(inner_one, down_1)
    resid_grad = top_grad + norm_back(resid, norm_gain[1], norm_bias[1], normed_two_grad)
    branch_grad = resid_grad.astype(BF)
    inner_o = product_back(branch_grad, up_a[3]).astype(BF)
    up_o_grad = outer_sum(rank_out, branch_grad)
    down_o_grad = outer_sum(inner_o, merged)
    merged_grad = product_back(branch_grad, attn_full[3]) + product_back(inner_o, down_a[3])
    merged_grad = merged_grad.astype(BF)
    early, owner = exchange(
        [down_2_grad, up_1_grad, up_2_grad, down_1_grad, down_o_grad, up_o_grad], devices, info=info
    )
    early, merged_grad, result = lax.optimization_barrier((early, merged_grad, result))
    early = place.gather_all(early)
    result = place.to_tokens(result, images)

    proj_grads = [grad.T for grad in attend_grads(*turned, log_total, merged_grad.T)]
    normed_grad = 0.0
    late_parts = []
    for index in range(3):
        inner = product_back(proj_grads[index], up_a[index]).astype(BF)
        late_parts.append(outer_sum(inner, normed))
        late_parts.append(outer_sum(rank_parts[index], proj_grads[index]))
        normed_grad = (
            normed_grad
            + product_back(proj_grads[index], attn_full[index])
            + product_back(inner, down_a[index])
        )
    late, _ = exchange(late_parts, devices, owner=owner)
    late = place.gather_all(late)
    input_grad = resid_grad + norm_back(flat, norm_gain[0], norm_bias[0], normed_grad)
    input_grad = place.to_tokens(input_grad.astype(BF), images).astype(F32)
    return (result, input_grad, *write_grads(early, late, width, hidden_size))


def solution(mesh):
    in_specs = (
        P("dp", "seq", None),
        P("dp", "seq", None),
        P("dp"),
        P("dp"),
        P("dp", None),
        P("seq", None, None),
        P("seq", None),
        P("seq", None),
        P("seq", None),
        P(),
        P(),
        P(),
        P(),
        P(),
        P(),
        P(),
        P(),
        P(),
        P(),
    )
    out_specs = (P("dp", "seq", None), P("dp", "seq", None), P(), P(), P(), P(), P(), P())

    def run(*args):
        return local(mesh.shape["dp"], mesh.shape["seq"], *args)

    return jax.shard_map(run, mesh=mesh, in_specs=in_specs, out_specs=out_specs, check_vma=False)
```
